128 devices in a mesh: head: 4 (over x_lo, core), blk: 32 (over x_hi, z, y).
Axes of the slice: x: 4 (x_hi: 2, x_lo: 2; x = x_hi * 2 + x_lo), y: 4, z: 4, core: 2. Of those that a mesh axis runs over, the one named last changes fastest.
Arguments:
- query: bfloat16 [16384, 32, 128], P(('blk', 'head')), may hold values from -12 to 12
- keys: bfloat16 [16384, 4, 128], P(('blk', 'head')), may hold values from -12 to 12
- values: bfloat16 [16384, 4, 128], P(('blk', 'head')), may hold values from -6 to 6
- output: bfloat16 [16384, 32, 128], P(('blk', 'head')), may hold values from -1.5 to 1.5
- dout: bfloat16 [16384, 32, 128], P(('blk', 'head')), may hold values from -192 to 192
Outputs:
- dquery: bfloat16 [16384, 32, 128], P(('blk', 'head'))
- dkeys: bfloat16 [16384, 4, 128], P(('blk', 'head'))
- dvalues: bfloat16 [16384, 4, 128], P(('blk', 'head'))
The draws below stay inside these ranges and needn't reach their ends.
All inputs are finite; a program needn't handle non-finite values.
Results may differ from the reference program's by a relative error of at most 0.01.
Values may be sent and summed in bfloat16 or wider, within the bound.
A program may use at most 192 MiB of HBM per device.

```python
import jax
import jax.numpy as jnp
from jax import lax

HEAD_SIZE = 128
QUERY_HEADS = 32
KEY_VALUE_HEADS = 4
BLOCK_TOKENS = 512
SEQUENCE_TOKENS = 16384
REACH = 4
N_BLK = 32


def draw_query(key, part):
    normalized_rows = jax.random.normal(jax.random.fold_in(key, 11), (SEQUENCE_TOKENS, QUERY_HEADS, HEAD_SIZE), jnp.float32)
    normalized_rows = jnp.clip(normalized_rows, -12.0, 12.0)
    return normalized_rows.astype(jnp.bfloat16)


def draw_keys(key, part):
    normalized_rows = jax.random.normal(jax.random.fold_in(key, 21), (SEQUENCE_TOKENS, KEY_VALUE_HEADS, HEAD_SIZE), jnp.float32)
    normalized_rows = jnp.clip(normalized_rows, -12.0, 12.0)
    return normalized_rows.astype(jnp.bfloat16)


def block_levels(key, dims, cuts, low, top_value):
    loudness, own = 1.0, jax.random.fold_in(key, 6)
    for axis_at, parts in cuts:
        draws = jnp.exp(jax.random.uniform(jax.random.fold_in(own, axis_at), (parts,), jnp.float32, low / len(cuts), top_value / len(cuts)))
        loudness = loudness * jnp.repeat(draws, dims[axis_at] // parts).reshape([-1 if axis == axis_at else 1 for axis in range(len(dims))])
    return loudness


def bell_draw(key, shape, deviation, limit, cuts=(), kind=jnp.bfloat16):
    result = jax.random.normal(key, shape, jnp.float32) * deviation
    if len(cuts) > 0:
        result = block_levels(key, shape, cuts, -0.22, 0.18) * result
    return jnp.clip(result, min=-limit, max=limit).astype(kind)


def setup_inputs(seed: int = 0) -> dict:
    key_of = jax.random.split(jax.random.key(seed), 6)
    return {
        "query": draw_query(jax.random.fold_in(key_of[5], 71), 0),
        "keys": draw_keys(jax.random.fold_in(key_of[5], 71), 0),
        "values": bell_draw(key_of[2], (SEQUENCE_TOKENS, KEY_VALUE_HEADS, HEAD_SIZE), 1.0, 6.0, ((0, 128),)),
        "output": bell_draw(key_of[3], (SEQUENCE_TOKENS, QUERY_HEADS, HEAD_SIZE), 0.25, 1.5, ((0, 128),)),
        "dout": bell_draw(key_of[4], (SEQUENCE_TOKENS, QUERY_HEADS, HEAD_SIZE), 32.0, 192.0, ((0, 128),)),
    }


def head_grads(items):
    query_rows, dout_rows, output_rows, key_rows, value_rows, living_mask = items
    scaling = HEAD_SIZE ** -0.5
    scores = jnp.einsum("qgd,kd->gqk", query_rows, key_rows) * scaling
    scores = jnp.where(living_mask[None, None, :], scores, -jnp.inf)
    row_max = jnp.max(scores, axis=-1, keepdims=True)
    logarithm_sum = row_max + jnp.log(jnp.sum(jnp.exp(scores - row_max), axis=-1, keepdims=True))
    probability_rows = jnp.exp(scores - logarithm_sum)
    probs_low = lax.optimization_barrier(probability_rows.astype(jnp.bfloat16)).astype(jnp.float32)
    delta_rows = jnp.sum(dout_rows * output_rows, axis=-1)
    delta_rows = lax.optimization_barrier(delta_rows.astype(jnp.bfloat16)).astype(jnp.float32)
    delta_rows = jnp.transpose(delta_rows, (1, 0))
    value_grad = jnp.einsum("gqk,qgd->kd", probs_low, dout_rows)
    prob_grad = jnp.einsum("qgd,kd->gqk", dout_rows, value_rows)
    score_grad = probability_rows * (prob_grad - delta_rows[:, :, None]) * scaling
    score_low = lax.optimization_barrier(score_grad.astype(jnp.bfloat16)).astype(jnp.float32)
    query_grad = jnp.einsum("gqk,kd->qgd", score_low, key_rows)
    key_grad = jnp.einsum("gqk,qgd->kd", score_low, query_rows)
    return query_grad.astype(jnp.bfloat16), key_grad, value_grad


def reference(query, keys, values, output, dout):
    query_group_count = QUERY_HEADS // KEY_VALUE_HEADS
    padding_amount = REACH * BLOCK_TOKENS
    neighbour_window = (2 * REACH + 1) * BLOCK_TOKENS
    key_pad = jnp.pad(keys.astype(jnp.float32), ((padding_amount, padding_amount), (0, 0), (0, 0)))
    value_pad = jnp.pad(values.astype(jnp.float32), ((padding_amount, padding_amount), (0, 0), (0, 0)))
    offsets = jnp.arange(neighbour_window, dtype=jnp.int32) // BLOCK_TOKENS - REACH

    def block_step(carry, index):
        key_acc, value_acc = carry
        start = (index * BLOCK_TOKENS).astype(jnp.int32)

        def grouped(array):
            block_portion = lax.dynamic_slice_in_dim(array, start, BLOCK_TOKENS, 0).astype(jnp.float32)
            return jnp.transpose(block_portion.reshape(BLOCK_TOKENS, KEY_VALUE_HEADS, query_group_count, HEAD_SIZE), (1, 0, 2, 3))

        key_rows = jnp.transpose(lax.dynamic_slice_in_dim(key_pad, start, neighbour_window, 0), (1, 0, 2))
        value_rows = jnp.transpose(lax.dynamic_slice_in_dim(value_pad, start, neighbour_window, 0), (1, 0, 2))
        neighbour = index + offsets
        living_mask = (neighbour >= 0) & (neighbour < N_BLK)
        living_heads = jnp.broadcast_to(living_mask[None, :], (KEY_VALUE_HEADS, neighbour_window))
        query_grad, key_grad, value_grad = lax.map(
            head_grads, (grouped(query), grouped(dout), grouped(output), key_rows, value_rows, living_heads))
        query_grad = jnp.transpose(query_grad, (1, 0, 2, 3)).reshape(BLOCK_TOKENS, QUERY_HEADS, HEAD_SIZE)
        key_grad = jnp.transpose(key_grad, (1, 0, 2))
        value_grad = jnp.transpose(value_grad, (1, 0, 2))
        key_acc = lax.dynamic_update_slice_in_dim(
            key_acc, lax.dynamic_slice_in_dim(key_acc, start, neighbour_window, 0) + key_grad, start, 0)
        value_acc = lax.dynamic_update_slice_in_dim(
            value_acc, lax.dynamic_slice_in_dim(value_acc, start, neighbour_window, 0) + value_grad, start, 0)
        return (key_acc, value_acc), query_grad

    zeroed_accumulator = jnp.zeros((SEQUENCE_TOKENS + 2 * padding_amount, KEY_VALUE_HEADS, HEAD_SIZE), jnp.float32)
    indices = jnp.arange(N_BLK, dtype=jnp.int32)
    (key_acc, value_acc), query_grad = lax.scan(block_step, (zeroed_accumulator, zeroed_accumulator), indices)
    dquery = query_grad.reshape(SEQUENCE_TOKENS, QUERY_HEADS, HEAD_SIZE)
    dkeys = key_acc[padding_amount:padding_amount + SEQUENCE_TOKENS].astype(jnp.bfloat16)
    dvalues = value_acc[padding_amount:padding_amount + SEQUENCE_TOKENS].astype(jnp.bfloat16)
    return dquery, dkeys, dvalues
```

```python
import functools
import math

import jax
import jax.numpy as jnp
from jax import lax
from jax.experimental import pallas as pl
from jax.experimental.pallas import tpu as pltpu
from jax.sharding import PartitionSpec as P

BF = jnp.bfloat16
F32 = jnp.float32
MINOR = (((1,), (1,)), ((), ()))
MESH = pl.DeviceIdType.MESH
ANY = pl.BlockSpec(memory_space=pl.ANY)
VMEM = pl.BlockSpec(memory_space=pltpu.VMEM)


class Dims:
    def __init__(self, query, keys, mesh):
        self.tokens, self.q_heads, self.width = query.shape
        self.kv_heads = keys.shape[1]
        self.n_head = mesh.shape["head"]
        self.n_blk = mesh.shape["blk"]
        self.reach = self.n_blk // 8
        self.slots = 2 * self.reach + 1
        self.block = self.tokens * self.n_head
        self.group = self.q_heads // self.n_head
        self.chunk = self.tokens * self.group
        self.rows = self.chunk * self.n_head
        self.scaling = self.width ** (-0.5)
        self.log2_scaling = self.scaling * math.log2(math.e)


def aligned(index, size):
    return pl.ds(pl.multiple_of(index * size, size), size)


def remote(src, dst, send, recv, head=None, blk=None):
    where = {}
    if head is not None:
        where["head"] = head
    if blk is not None:
        where["blk"] = blk
    return pltpu.make_async_remote_copy(
        src_ref=src, dst_ref=dst, send_sem=send, recv_sem=recv, device_id=where, device_id_type=MESH
    )


def each_neighbour(dm, position, body):
    for distance in range(1, dm.reach + 1):
        for offset in (distance, -distance):
            other = position + offset

            @pl.when((other >= 0) & (other < dm.n_blk))
            def _():
                body(offset)


def meet(dm, me, position):
    barrier = pltpu.get_barrier_semaphore()
    for step in range(1, dm.n_head):
        pl.semaphore_signal(
            barrier, inc=1, device_id={"head": lax.rem(me + step, dm.n_head)}, device_id_type=MESH
        )
    each_neighbour(
        dm,
        position,
        lambda offset: pl.semaphore_signal(
            barrier, inc=1, device_id={"blk": position + offset}, device_id_type=MESH
        ),
    )
    before = jnp.minimum(position, dm.reach)
    after = jnp.minimum(dm.n_blk - 1 - position, dm.reach)
    pl.semaphore_wait(barrier, dm.n_head - 1 + before + after)


def split_heads(dm, source, staged, wide, part):
    wide[...] = source[...].astype(F32)
    for g in range(dm.n_head):
        staged[g, part] = wide[pl.ds(g, dm.tokens, stride=dm.kv_heads), :].astype(BF)


def delta_rows(dm, dout, output, rows):
    ones = jnp.ones((8, dm.width), BF)
    for g in range(dm.n_head):
        heads = slice(g * dm.group, (g + 1) * dm.group)
        product = dout[:, heads, :].astype(F32) * output[:, heads, :].astype(F32)
        product = product.reshape(dm.chunk, dm.width)
        high = product.astype(BF)
        low = (product - high.astype(F32)).astype(BF)
        total = lax.dot_general(ones, high, MINOR, preferred_element_type=F32) + lax.dot_general(
            ones, low, MINOR, preferred_element_type=F32
        )
        rows[g] = total[0:1, :].astype(BF).astype(F32)


def gather_kernel(dm, query, dout, dout_v, output_v, keys, values, q_out, do_out, delta_out, kv_out,
                  staged, wide, drow, local, s_kv, r_kv, s_q, r_q, s_do, r_do, s_de, r_de, s_n, r_n):
    me = lax.axis_index("head")
    position = lax.axis_index("blk")
    split_heads(dm, keys, staged, wide, 0)
    split_heads(dm, values, staged, wide, 1)
    delta_rows(dm, dout_v, output_v, drow)
    meet(dm, me, position)

    def group(ref, g):
        return ref.at[:, aligned(g, dm.group), :]

    def kv_copy(g, sem, to):
        return remote(staged.at[g], kv_out.at[dm.reach, :, aligned(sem, dm.tokens), :],
                      s_kv.at[g], r_kv.at[sem], head=to)

    def q_copy(g, sem, to):
        return remote(group(query, g), q_out.at[sem], s_q.at[g], r_q.at[sem], head=to)

    def do_copy(g, sem, to):
        return remote(group(dout, g), do_out.at[sem], s_do.at[g], r_do.at[sem], head=to)

    def de_copy(g, sem, to):
        return remote(drow.at[g], delta_out.at[sem], s_de.at[g], r_de.at[sem], head=to)

    peers = [lax.rem(me + step, dm.n_head) for step in range(1, dm.n_head)]
    for make in (kv_copy, de_copy, q_copy, do_copy):
        for g in peers:
            make(g, me, g).start()
    own = [
        pltpu.make_async_copy(staged.at[me], kv_out.at[dm.reach, :, aligned(me, dm.tokens), :], local.at[0]),
        pltpu.make_async_copy(group(query, me), q_out.at[me], local.at[1]),
        pltpu.make_async_copy(group(dout, me), do_out.at[me], local.at[2]),
        pltpu.make_async_copy(drow.at[me], delta_out.at[me], local.at[3]),
    ]
    for copy in own:
        copy.start()
    own[0].wait()
    for g in peers:
        kv_copy(me, g, g).wait_recv()

    def neighbour(offset, slot):
        return remote(kv_out.at[dm.reach], kv_out.at[slot], s_n.at[dm.reach + offset], r_n.at[slot],
                      blk=position + offset)

    each_neighbour(dm, position, lambda offset: neighbour(offset, dm.reach - offset).start())
    for copy in own[1:]:
        copy.wait()
    for make in (kv_copy, de_copy, q_copy, do_copy):
        for g in peers:
            make(g, me, g).wait_send()
            if make is not kv_copy:
                make(me, g, g).wait_recv()
    each_neighbour(dm, position, lambda offset: neighbour(offset, dm.reach - offset).wait_send())
    each_neighbour(dm, position, lambda offset: neighbour(offset, dm.reach + offset).wait_recv())


def gather(dm, query, keys, values, output, dout):
    n, dma = dm.n_head, pltpu.SemaphoreType.DMA
    return pl.pallas_call(
        functools.partial(gather_kernel, dm),
        out_shape=(
            jax.ShapeDtypeStruct((n, dm.tokens, dm.group, dm.width), BF),
            jax.ShapeDtypeStruct((n, dm.tokens, dm.group, dm.width), BF),
            jax.ShapeDtypeStruct((n, 1, dm.chunk), F32),
            jax.ShapeDtypeStruct((dm.slots, 2, dm.block, dm.width), BF),
        ),
        in_specs=[ANY, ANY, VMEM, VMEM, VMEM, VMEM],
        out_specs=[ANY] * 4,
        scratch_shapes=[
            pltpu.VMEM((n, 2, dm.tokens, dm.width), BF),
            pltpu.VMEM((dm.tokens * dm.kv_heads, dm.width), F32),
            pltpu.VMEM((n, 1, dm.chunk), F32),
            dma((4,)),
        ]
        + [dma((n,))] * 8
        + [dma((dm.slots,))] * 2,
        compiler_params=pltpu.CompilerParams(
            collective_id=0, has_side_effects=True, vmem_limit_bytes=32 * 2**20
        ),
        name="gather_heads",
    )(
        query,
        dout,
        dout,
        output,
        keys.reshape(dm.tokens * dm.kv_heads, dm.width),
        values.reshape(dm.tokens * dm.kv_heads, dm.width),
    )


def score_phase(dm, keys, q_t, probs, scores, tops, sums, b, tile):
    block, width = dm.block, dm.log2_scaling
    count = dm.rows // tile
    for i in range(count + 1):
        if i < count:
            columns = slice(i * tile, (i + 1) * tile)
            scores[i % 2] = jnp.dot(keys, q_t[:, columns], preferred_element_type=F32)
        if i > 0:
            columns = slice((i - 1) * tile, i * tile)
            x = scores[(i - 1) % 2]
            top = jnp.max(jnp.max(x.reshape(block // 8, 8, tile), axis=0), axis=0, keepdims=True)
            p = jnp.exp2((x - top) * width)
            total = jnp.sum(jnp.sum(p.reshape(block // 8, 8, tile), axis=0), axis=0, keepdims=True)
            probs[aligned(b, block), columns] = p.astype(BF)
            tops[pl.ds(b, 1), columns] = top
            sums[pl.ds(b, 1), columns] = total


def combine(dm, tops, sums, factors):
    top = tops[...]
    weight = jnp.exp2((top - jnp.max(top, axis=0, keepdims=True)) * dm.log2_scaling)
    factors[...] = weight / jnp.sum(weight * sums[...], axis=0, keepdims=True)


def gradient_phase(dm, keys_t, values, q_t, do_t, delta, probs, factors, dq_t, small, b, tile):
    block = dm.block
    count = dm.rows // tile
    per_chunk = dm.chunk // tile
    rows = aligned(b, block)
    dk = jnp.zeros((dm.width, block), F32)
    dv = jnp.zeros((dm.width, block), F32)
    for i in range(count + 1):
        if i < count:
            columns = slice(i * tile, (i + 1) * tile)
            inner = slice((i % per_chunk) * tile, (i % per_chunk + 1) * tile)
            prob_grad = jnp.dot(values, do_t[:, columns], preferred_element_type=F32)
            grad = probs[rows, columns].astype(F32) * (prob_grad - delta[i // per_chunk, :, inner])
            small[i % 2] = grad.astype(BF)
        if i > 0:
            columns = slice((i - 1) * tile, i * tile)
            factor = factors[pl.ds(b, 1), columns]
            scaled = factor * dm.scaling
            grad = small[(i - 1) % 2]
            do_scaled = (do_t[:, columns].astype(F32) * factor).astype(BF)
            q_scaled = (q_t[:, columns].astype(F32) * scaled).astype(BF)
            dv = dv + lax.dot_general(do_scaled, probs[rows, columns], MINOR, preferred_element_type=F32)
            dk = dk + lax.dot_general(q_scaled, grad, MINOR, preferred_element_type=F32)
            dq_t[:, columns] += jnp.dot(keys_t, grad, preferred_element_type=F32) * scaled
    return dk, dv


def attention_kernel(dm, q, do, delta, kv, dq, dkv, keys_t, q_t, do_t, probs, scores, small, tops, sums,
                     factors, dq_t):
    position = lax.axis_index("blk")
    low = jnp.maximum(dm.reach - position, 0)
    high = jnp.minimum(dm.slots, dm.n_blk + dm.reach - position)
    step = 512
    for at in range(0, dm.rows, step):
        columns = slice(at, at + step)
        q_t[:, columns] = q[columns, :].T
        do_t[:, columns] = do[columns, :].T
        dq_t[:, columns] = jnp.zeros((dm.width, step), F32)
    tops[...] = jnp.full((dm.slots, dm.rows), -jnp.inf, F32)
    sums[...] = jnp.zeros((dm.slots, dm.rows), F32)

    @pl.loop(low, high)
    def _(b):
        keys_t[:, aligned(b, dm.block)] = kv[b, 0].T
        score_phase(dm, kv[b, 0], q_t, probs, scores, tops, sums, b, 512)

    combine(dm, tops, sums, factors)

    @pl.loop(low, high)
    def _(b):
        dk, dv = gradient_phase(
            dm, keys_t[:, aligned(b, dm.block)], kv[b, 1], q_t, do_t, delta, probs, factors, dq_t, small, b, 256
        )
        dkv[b, 0] = dk.astype(BF)
        dkv[b, 1] = dv.astype(BF)

    for at in range(0, dm.rows, step):
        columns = slice(at, at + step)
        dq[columns, :] = dq_t[:, columns].T.astype(BF)


def attention(dm, q, do, delta, kv):
    span = dm.slots * dm.block
    return pl.pallas_call(
        functools.partial(attention_kernel, dm),
        out_shape=(
            jax.ShapeDtypeStruct((dm.rows, dm.width), BF),
            jax.ShapeDtypeStruct((dm.slots, 2, dm.width, dm.block), BF),
        ),
        in_specs=[VMEM] * 4,
        out_specs=[VMEM] * 2,
        scratch_shapes=[
            pltpu.VMEM((dm.width, span), BF),
            pltpu.VMEM((dm.width, dm.rows), BF),
            pltpu.VMEM((dm.width, dm.rows), BF),
            pltpu.VMEM((span, dm.rows), BF),
            pltpu.VMEM((2, dm.block, 512), F32),
            pltpu.VMEM((2, dm.block, 256), BF),
            pltpu.VMEM((dm.slots, dm.rows), F32),
            pltpu.VMEM((dm.slots, dm.rows), F32),
            pltpu.VMEM((dm.slots, dm.rows), F32),
            pltpu.VMEM((dm.width, dm.rows), F32),
        ],
        compiler_params=pltpu.CompilerParams(vmem_limit_bytes=60 * 2**20),
        name="attention_gradients",
    )(q, do, delta, kv)


def scatter_kernel(dm, dq, dkv, dquery, dkeys, dvalues, received, total, heads, wide,
                   local, s_q, r_q, s_n, r_n, s_kv, r_kv):
    me = lax.axis_index("head")
    position = lax.axis_index("blk")
    meet(dm, me, position)
    peers = [lax.rem(me + step, dm.n_head) for step in range(1, dm.n_head)]

    def neighbour(offset, slot):
        return remote(dkv.at[dm.reach + offset], received.at[slot], s_n.at[dm.reach + offset], r_n.at[slot],
                      blk=position + offset)

    def dq_copy(g, sem, to):
        return remote(dq.at[g], dquery.at[:, aligned(sem, dm.group), :], s_q.at[g], r_q.at[sem], head=to)

    each_neighbour(dm, position, lambda offset: neighbour(offset, dm.reach - offset).start())
    for g in peers:
        dq_copy(g, me, g).start()
    own = pltpu.make_async_copy(dq.at[me], dquery.at[:, aligned(me, dm.group), :], local.at[0])
    own.start()
    mine = pltpu.make_async_copy(dkv.at[dm.reach], received.at[dm.reach], local.at[1])
    mine.start()
    mine.wait()
    total[...] = received[dm.reach].astype(F32)

    def add(offset):
        neighbour(offset, dm.reach + offset).wait_recv()
        total[...] += received[dm.reach + offset].astype(F32)

    each_neighbour(dm, position, add)
    for part in range(2):
        rows = total[part].T.astype(BF)
        for g in range(dm.n_head):
            heads[g, part] = rows[g * dm.tokens:(g + 1) * dm.tokens, :]

    return peers, own, neighbour, dq_copy


def scatter_all(dm, dq, dkv, dquery, dkeys, dvalues, received, total, heads, landed, wide,
                local, s_q, r_q, s_n, r_n, s_kv, r_kv):
    me = lax.axis_index("head")
    position = lax.axis_index("blk")
    peers, own, neighbour, dq_copy = scatter_kernel(
        dm, dq, dkv, dquery, dkeys, dvalues, received, total, heads, wide, local, s_q, r_q, s_n, r_n, s_kv, r_kv
    )

    def kv_copy(g, sem, to):
        return remote(heads.at[g], landed.at[sem], s_kv.at[g], r_kv.at[sem], head=to)

    for g in peers:
        kv_copy(g, me, g).start()
    mine = pltpu.make_async_copy(heads.at[me], landed.at[me], local.at[1])
    mine.start()
    mine.wait()
    for g in peers:
        kv_copy(me, g, g).wait_recv()
    for part, out in ((0, dkeys), (1, dvalues)):
        for g in range(dm.n_head):
            wide[pl.ds(g, dm.tokens, stride=dm.kv_heads), :] = landed[g, part].astype(F32)
        out[...] = wide[...].astype(BF)
    own.wait()
    for g in peers:
        kv_copy(g, me, g).wait_send()
        dq_copy(g, me, g).wait_send()
        dq_copy(me, g, g).wait_recv()
    each_neighbour(dm, position, lambda offset: neighbour(offset, dm.reach - offset).wait_send())


def scatter(dm, dq, dkv):
    n, dma = dm.n_head, pltpu.SemaphoreType.DMA
    flat = dm.tokens * dm.kv_heads
    return pl.pallas_call(
        functools.partial(scatter_all, dm),
        out_shape=(
            jax.ShapeDtypeStruct((dm.tokens, dm.q_heads, dm.width), BF),
            jax.ShapeDtypeStruct((flat, dm.width), BF),
            jax.ShapeDtypeStruct((flat, dm.width), BF),
        ),
        in_specs=[ANY, ANY],
        out_specs=[ANY, VMEM, VMEM],
        scratch_shapes=[
            pltpu.VMEM((dm.slots, 2, dm.width, dm.block), BF),
            pltpu.VMEM((2, dm.width, dm.block), F32),
            pltpu.VMEM((n, 2, dm.tokens, dm.width), BF),
            pltpu.VMEM((n, 2, dm.tokens, dm.width), BF),
            pltpu.VMEM((flat, dm.width), F32),
            dma((2,)),
            dma((n,)),
            dma((n,)),
            dma((dm.slots,)),
            dma((dm.slots,)),
            dma((n,)),
            dma((n,)),
        ],
        compiler_params=pltpu.CompilerParams(
            collective_id=1, has_side_effects=True, vmem_limit_bytes=32 * 2**20
        ),
        name="return_gradients",
    )(dq, dkv)


def solution(mesh):
    def on_device(query, keys, values, output, dout):
        dm = Dims(query, keys, mesh)
        q, do, delta, kv = gather(dm, query, keys, values, output, dout)
        dq, dkv = attention(dm, q.reshape(dm.rows, dm.width), do.reshape(dm.rows, dm.width), delta, kv)
        dquery, dkeys, dvalues = scatter(dm, dq.reshape(dm.n_head, dm.tokens, dm.group, dm.width), dkv)
        return dquery, dkeys.reshape(keys.shape), dvalues.reshape(values.shape)

    spec = P(("blk", "head"), None, None)
    return jax.shard_map(
        on_device, mesh=mesh, in_specs=(spec,) * 5, out_specs=(spec,) * 3, check_vma=False
    )
```

```python
import functools
import math

import jax
import jax.numpy as jnp
from jax import lax
from jax.experimental import pallas as pl
from jax.experimental.pallas import tpu as pltpu
from jax.sharding import PartitionSpec as P

BF = jnp.bfloat16
F32 = jnp.float32
MINOR = (((1,), (1,)), ((), ()))
MESH = pl.DeviceIdType.MESH
ANY = pl.BlockSpec(memory_space=pl.ANY)
VMEM = pl.BlockSpec(memory_space=pltpu.VMEM)


class Dims:
    def __init__(self, query, keys, mesh):
        self.tokens, self.q_heads, self.width = query.shape
        self.kv_heads = keys.shape[1]
        self.n_head = mesh.shape["head"]
        self.n_blk = mesh.shape["blk"]
        self.reach = self.n_blk // 8
        self.slots = 2 * self.reach + 1
        self.block = self.tokens * self.n_head
        self.group = self.q_heads // self.n_head
        self.chunk = self.tokens * self.group
        self.rows = self.chunk * self.n_head
        self.scaling = self.width ** (-0.5)
        self.log2_scaling = self.scaling * math.log2(math.e)
        self.score_tile = 512
        self.grad_tile = 256


def aligned(index, size):
    return pl.ds(pl.multiple_of(index * size, size), size)


def remote(src, dst, send, recv, head=None, blk=None):
    where = {}
    if head is not None:
        where["head"] = head
    if blk is not None:
        where["blk"] = blk
    return pltpu.make_async_remote_copy(
        src_ref=src, dst_ref=dst, send_sem=send, recv_sem=recv, device_id=where, device_id_type=MESH
    )


def split_heads(dm, source, staged, wide, part):
    wide[...] = source[...].astype(F32)
    for g in range(dm.n_head):
        staged[g, part] = wide[pl.ds(g, dm.tokens, stride=dm.kv_heads), :].astype(BF)


def delta_rows(dm, dout, output, rows):
    ones = jnp.ones((8, dm.width), BF)
    for g in range(dm.n_head):
        heads = slice(g * dm.group, (g + 1) * dm.group)
        product = dout[:, heads, :].astype(F32) * output[:, heads, :].astype(F32)
        product = product.reshape(dm.chunk, dm.width)
        high = product.astype(BF)
        low = (product - high.astype(F32)).astype(BF)
        total = lax.dot_general(ones, high, MINOR, preferred_element_type=F32) + lax.dot_general(
            ones, low, MINOR, preferred_element_type=F32
        )
        rows[g] = total[0:1, :].astype(BF).astype(F32)


def score_phase(dm, keys, q_t, probs, scores, tops, sums, b, first, count):
    block, tile = dm.block, dm.score_tile
    for i in range(count + 1):
        if i < count:
            columns = aligned(first + i, tile)
            scores[i % 2] = jnp.dot(keys, q_t[:, columns], preferred_element_type=F32)
        if i > 0:
            columns = aligned(first + i - 1, tile)
            x = scores[(i - 1) % 2]
            top = jnp.max(jnp.max(x.reshape(block // 8, 8, tile), axis=0), axis=0, keepdims=True)
            p = jnp.exp2((x - top) * dm.log2_scaling)
            total = jnp.sum(jnp.sum(p.reshape(block // 8, 8, tile), axis=0), axis=0, keepdims=True)
            probs[aligned(b, block), columns] = p.astype(BF)
            tops[pl.ds(b, 1), columns] = top
            sums[pl.ds(b, 1), columns] = total


def combine(dm, tops, sums, factors):
    top = tops[...]
    weight = jnp.exp2((top - jnp.max(top, axis=0, keepdims=True)) * dm.log2_scaling)
    factors[...] = weight / jnp.sum(weight * sums[...], axis=0, keepdims=True)


def gradient_phase(dm, keys_t, values, q_t, do_t, delta, probs, factors, dq_t, small, b):
    block, tile = dm.block, dm.grad_tile
    count = dm.rows // tile
    per_chunk = dm.chunk // tile
    rows = aligned(b, block)
    dk = jnp.zeros((dm.width, block), F32)
    dv = jnp.zeros((dm.width, block), F32)
    for i in range(count + 1):
        if i < count:
            columns = slice(i * tile, (i + 1) * tile)
            inner = slice((i % per_chunk) * tile, (i % per_chunk + 1) * tile)
            prob_grad = jnp.dot(values, do_t[:, columns], preferred_element_type=F32)
            grad = probs[rows, columns].astype(F32) * (prob_grad - delta[i // per_chunk, :, inner])
            small[i % 2] = grad.astype(BF)
        if i > 0:
            columns = slice((i - 1) * tile, i * tile)
            factor = factors[pl.ds(b, 1), columns]
            scaled = factor * dm.scaling
            grad = small[(i - 1) % 2]
            do_scaled = (do_t[:, columns].astype(F32) * factor).astype(BF)
            q_scaled = (q_t[:, columns].astype(F32) * scaled).astype(BF)
            dv = dv + lax.dot_general(do_scaled, probs[rows, columns], MINOR, preferred_element_type=F32)
            dk = dk + lax.dot_general(q_scaled, grad, MINOR, preferred_element_type=F32)
            dq_t[:, columns] += jnp.dot(keys_t, grad, preferred_element_type=F32) * scaled
    return dk, dv


def kernel(dm, query, dout, output, keys, values, dquery, dkeys, dvalues,
           staged, wide, drow, dout_v, output_v, q_in, do_in, delta, kv,
           keys_t, q_t, do_t, probs, scores, small, tops, sums, factors, dq_t,
           dkv, inbox, relay, upright, total, heads, landed, dq,
           local, s_kv, r_kv, s_q, r_q, s_do, r_do, s_de, r_de, s_near, s_far, s_pass, r_n,
           s_in, r_in, s_up, r_up, s_dq, r_dq, s_h, r_h):
    me = lax.axis_index("head")
    position = lax.axis_index("blk")
    n, w = dm.n_head, dm.reach
    place = lax.rem(position, w)
    pair = me // 2
    core = lax.rem(me, 2)
    mate = pair * 2 + 1 - core
    across = [(1 - pair) * 2 + core, (1 - pair) * 2 + 1 - core]
    peers = across + [mate]
    has_before = position - w >= 0
    has_after = position + w < dm.n_blk
    others = [lax.rem(place + s, w) for s in range(1, w)]

    own = [
        pltpu.make_async_copy(dout, dout_v, local.at[0]),
        pltpu.make_async_copy(output, output_v, local.at[1]),
        pltpu.make_async_copy(query.at[:, aligned(me, dm.group), :], q_in.at[me], local.at[2]),
        pltpu.make_async_copy(dout.at[:, aligned(me, dm.group), :], do_in.at[me], local.at[3]),
    ]
    for copy in own:
        copy.start()
    barrier = pltpu.get_barrier_semaphore()
    for g in peers:
        pl.semaphore_signal(barrier, inc=1, device_id={"head": g}, device_id_type=MESH)
    for c in others:
        pl.semaphore_signal(barrier, inc=1, device_id={"blk": position + c - place}, device_id_type=MESH)

    @pl.when(has_before)
    def _():
        pl.semaphore_signal(barrier, inc=1, device_id={"blk": position - w}, device_id_type=MESH)

    @pl.when(has_after)
    def _():
        pl.semaphore_signal(barrier, inc=1, device_id={"blk": position + w}, device_id_type=MESH)

    split_heads(dm, keys, staged, wide, 0)
    split_heads(dm, values, staged, wide, 1)
    groups = position // w
    ends = jnp.minimum(groups, 1) + jnp.minimum(dm.n_blk // w - 1 - groups, 1)
    pl.semaphore_wait(barrier, n - 1 + w - 1 + ends)

    def kv_copy(g, source, to):
        return remote(staged.at[g], kv.at[w, :, aligned(source, dm.tokens), :], s_kv.at[g], r_kv.at[source], head=to)

    def q_copy(g, source, to):
        return remote(query.at[:, aligned(g, dm.group), :], q_in.at[source], s_q.at[g], r_q.at[source], head=to)

    def do_copy(g, source, to):
        return remote(dout.at[:, aligned(g, dm.group), :], do_in.at[source], s_do.at[g], r_do.at[source], head=to)

    def de_copy(g, source, to):
        return remote(drow.at[g], delta.at[source], s_de.at[g], r_de.at[source], head=to)

    for make in (kv_copy, q_copy):
        for g in peers:
            make(g, me, g).start()
    kv_own = pltpu.make_async_copy(staged.at[me], kv.at[w, :, aligned(me, dm.tokens), :], local.at[4])
    kv_own.start()
    own[0].wait()
    own[1].wait()
    delta_rows(dm, dout_v, output_v, drow)
    for g in peers:
        de_copy(g, me, g).start()
    de_own = pltpu.make_async_copy(drow.at[me], delta.at[me], local.at[5])
    de_own.start()
    kv_own.wait()
    for g in peers:
        kv_copy(me, g, g).wait_recv()

    def near(c):
        return remote(kv.at[w], kv.at[w + place - c], s_near.at[c], r_n.at[w + place - c], blk=position + c - place)

    def far(step, side):
        slot = w - step
        return remote(kv.at[w], kv.at[slot], s_far.at[side], r_n.at[slot], blk=position + step)

    def passed(c, source):
        slot = lax.rem(place - c + 2 * w, 2 * w)
        return remote(kv.at[source], kv.at[slot], s_pass.at[c], r_n.at[slot], blk=position + c - place)

    @pl.when(has_before)
    def _():
        far(-w, 0).start()

    @pl.when(has_after)
    def _():
        far(w, 1).start()

    for c in others:
        near(c).start()

    for at in range(0, dm.rows, 512):
        dq_t[:, at:at + 512] = jnp.zeros((dm.width, 512), F32)
    tops[...] = jnp.full((dm.slots, dm.rows), -jnp.inf, F32)
    sums[...] = jnp.zeros((dm.slots, dm.rows), F32)

    def turn(source, target, g):
        target[:, aligned(g, dm.chunk)] = source[g].astype(F32).reshape(dm.chunk, dm.width).T.astype(BF)

    own[2].wait()
    turn(q_in, q_t, me)
    q_copy(me, mate, mate).wait_recv()
    turn(q_in, q_t, mate)

    def exists(slot):
        other = position - w + slot
        return (other >= 0) & (other < dm.n_blk)

    def arrival(j):
        kind, s = j // (w - 1), lax.rem(j, w - 1) + 1
        apart = lax.rem(place + s, w) - place
        side = lax.rem(w * s, 3 * w)
        inner = lax.rem(w * (2 - kind) + apart + 2 * w, 2 * w)
        return jnp.where(kind == 0, side, inner)

    half = dm.rows // 2 // dm.score_tile

    @pl.loop(0, dm.slots)
    def _(j):
        slot = arrival(j)

        @pl.when(exists(slot))
        def _():
            @pl.when(j > 0)
            def _():
                remote(kv.at[w], kv.at[slot], s_far.at[0], r_n.at[slot], head=mate).wait_recv()

            @pl.when((j == 1) & has_after)
            def _():
                for c in range(w):
                    @pl.when(c > place)
                    def _():
                        passed(c, 2 * w).start()

            @pl.when((j == 2) & has_before)
            def _():
                for c in range(w):
                    @pl.when(c < place)
                    def _():
                        passed(c, 0).start()

            keys_t[:, aligned(slot, dm.block)] = kv[slot, 0].T
            score_phase(dm, kv[slot, 0], q_t, probs, scores, tops, sums, slot, pair * half, half)

        @pl.when(j == 4)
        def _():
            for g in peers:
                do_copy(g, me, g).start()

    for g in across:
        q_copy(me, g, g).wait_recv()
        turn(q_in, q_t, g)

    @pl.loop(0, dm.slots)
    def _(slot):
        @pl.when(exists(slot))
        def _():
            score_phase(dm, kv[slot, 0], q_t, probs, scores, tops, sums, slot, (1 - pair) * half, half)

    combine(dm, tops, sums, factors)
    own[3].wait()
    turn(do_in, do_t, me)
    de_own.wait()
    for g in [mate] + across:
        do_copy(me, g, g).wait_recv()
        de_copy(me, g, g).wait_recv()
        turn(do_in, do_t, g)

    def to_member(direct, c):
        apart = c - place
        slot = w + apart if direct else lax.rem(apart + 2 * w, 2 * w)
        box = w * direct
        return remote(dkv.at[slot], inbox.at[box + place], s_in.at[box + c], r_in.at[box + place], blk=position + apart)

    def from_member(direct, c):
        box = w * direct
        return remote(dkv.at[w], inbox.at[box + c], s_in.at[box + c], r_in.at[box + c], blk=position + c - place)

    def to_side(side):
        step = w if side else -w
        return remote(relay.at[side], upright.at[1 - side], s_up.at[side], r_up.at[1 - side], blk=position + step)

    def from_side(side):
        step = w if side else -w
        return remote(relay.at[side], upright.at[side], s_up.at[side], r_up.at[side], blk=position + step)

    def gather_side(side):
        relay_sum = dkv[2 * w * side].astype(F32)
        total[...] = relay_sum
        for c in range(w):
            member = (c > place) if side else (c < place)

            @pl.when(member)
            def _():
                from_member(0, c).wait_recv()
                total[...] += inbox[c].astype(F32)

        relay[side] = total[...].astype(BF)
        to_side(side).start()

    def departure(j):
        s = jnp.where(j < w - 1, j + 1, j - w)
        apart = lax.rem(place + s, w) - place
        return jnp.where(
            j < w - 1,
            lax.rem(apart + 2 * w, 2 * w),
            jnp.where(j < w + 1, (j - w + 1) * 2 * w, jnp.where(j < 2 * w, w + apart, w)),
        )

    @pl.loop(0, dm.slots)
    def _(j):
        slot = departure(j)

        @pl.when(exists(slot))
        def _():
            dk, dv = gradient_phase(
                dm, keys_t[:, aligned(slot, dm.block)], kv[slot, 1], q_t, do_t, delta, probs, factors, dq_t, small, slot
            )
            dkv[slot, 0] = dk.astype(BF)
            dkv[slot, 1] = dv.astype(BF)

            @pl.when(j < w - 1)
            def _():
                to_member(0, lax.rem(place + j + 1, w)).start()

            @pl.when((j > w) & (j < 2 * w))
            def _():
                to_member(1, lax.rem(place + j - w + 2 * w, w)).start()

        @pl.when((j == w + 1) & has_before)
        def _():
            gather_side(0)

        @pl.when((j == w + 2) & has_after)
        def _():
            gather_side(1)

    def dq_copy(g, source, to):
        return remote(dq.at[g], dquery.at[:, aligned(source, dm.group), :], s_dq.at[g], r_dq.at[source], head=to)

    for g in peers + [me]:
        dq[g] = dq_t[:, aligned(g, dm.chunk)].T.reshape(dm.tokens, dm.group, dm.width).astype(BF)
        if g is not me:
            dq_copy(g, me, g).start()
    dq_own = pltpu.make_async_copy(dq.at[me], dquery.at[:, aligned(me, dm.group), :], local.at[6])
    dq_own.start()

    total[...] = dkv[w].astype(F32)
    for c in others:
        from_member(1, c).wait_recv()
        total[...] += inbox[w + c].astype(F32)

    @pl.when(has_before)
    def _():
        from_side(0).wait_recv()
        total[...] += upright[0].astype(F32)

    @pl.when(has_after)
    def _():
        from_side(1).wait_recv()
        total[...] += upright[1].astype(F32)

    for part in range(2):
        rows = total[part].T.astype(BF)
        for g in range(n):
            heads[g, part] = rows[g * dm.tokens:(g + 1) * dm.tokens, :]

    def head_copy(g, source, to):
        return remote(heads.at[g], landed.at[source], s_h.at[g], r_h.at[source], head=to)

    for g in peers:
        head_copy(g, me, g).start()
    head_own = pltpu.make_async_copy(heads.at[me], landed.at[me], local.at[7])
    head_own.start()
    head_own.wait()
    for g in peers:
        head_copy(me, g, g).wait_recv()
    for part, out in ((0, dkeys), (1, dvalues)):
        for g in range(n):
            wide[pl.ds(g, dm.tokens, stride=dm.kv_heads), :] = landed[g, part].astype(F32)
        out[...] = wide[...].astype(BF)

    dq_own.wait()
    for g in peers:
        for make in (kv_copy, q_copy, do_copy, de_copy, dq_copy, head_copy):
            make(g, me, g).wait_send()
        dq_copy(me, g, g).wait_recv()
    for c in others:
        near(c).wait_send()
        to_member(1, c).wait_send()

    @pl.when(has_before)
    def _():
        far(-w, 0).wait_send()
        to_side(0).wait_send()

    @pl.when(has_after)
    def _():
        far(w, 1).wait_send()
        to_side(1).wait_send()

    for c in range(w):

        @pl.when(has_before & (c < place))
        def _():
            passed(c, 0).wait_send()

        @pl.when(has_after & (c > place))
        def _():
            passed(c, 2 * w).wait_send()

        @pl.when(has_after & (c < place))
        def _():
            to_member(0, c).wait_send()

        @pl.when(has_before & (c > place))
        def _():
            to_member(0, c).wait_send()


def fused(dm, query, keys, values, output, dout):
    n, w, dma = dm.n_head, dm.reach, pltpu.SemaphoreType.DMA
    flat = dm.tokens * dm.kv_heads
    span = dm.slots * dm.block
    chunked = (n, dm.tokens, dm.group, dm.width)
    terms = (2, dm.width, dm.block)
    return pl.pallas_call(
        functools.partial(kernel, dm),
        out_shape=(
            jax.ShapeDtypeStruct(query.shape, BF),
            jax.ShapeDtypeStruct((flat, dm.width), BF),
            jax.ShapeDtypeStruct((flat, dm.width), BF),
        ),
        in_specs=[ANY, ANY, ANY, VMEM, VMEM],
        out_specs=[ANY, VMEM, VMEM],
        scratch_shapes=[
            pltpu.VMEM((n, 2, dm.tokens, dm.width), BF),
            pltpu.VMEM((flat, dm.width), F32),
            pltpu.VMEM((n, 1, dm.chunk), F32),
            pltpu.VMEM(query.shape, BF),
            pltpu.VMEM(query.shape, BF),
            pltpu.VMEM(chunked, BF),
            pltpu.VMEM(chunked, BF),
            pltpu.VMEM((n, 1, dm.chunk), F32),
            pltpu.VMEM((dm.slots, 2, dm.block, dm.width), BF),
            pltpu.VMEM((dm.width, span), BF),
            pltpu.VMEM((dm.width, dm.rows), BF),
            pltpu.VMEM((dm.width, dm.rows), BF),
            pltpu.VMEM((span, dm.rows), BF),
            pltpu.VMEM((2, dm.block, dm.score_tile), F32),
            pltpu.VMEM((2, dm.block, dm.grad_tile), BF),
            pltpu.VMEM((dm.slots, dm.rows), F32),
            pltpu.VMEM((dm.slots, dm.rows), F32),
            pltpu.VMEM((dm.slots, dm.rows), F32),
            pltpu.VMEM((dm.width, dm.rows), F32),
            pltpu.VMEM((dm.slots,) + terms, BF),
            pltpu.VMEM((2 * w,) + terms, BF),
            pltpu.VMEM((2,) + terms, BF),
            pltpu.VMEM((2,) + terms, BF),
            pltpu.VMEM(terms, F32),
            pltpu.VMEM((n, 2, dm.tokens, dm.width), BF),
            pltpu.VMEM((n, 2, dm.tokens, dm.width), BF),
            pltpu.VMEM(chunked, BF),
            dma((8,)),
        ]
        + [dma((n,))] * 8
        + [dma((w,)), dma((2,)), dma((w,)), dma((dm.slots,))]
        + [dma((2 * w,)), dma((2 * w,)), dma((2,)), dma((2,))]
        + [dma((n,))] * 4,
        compiler_params=pltpu.CompilerParams(
            collective_id=0, has_side_effects=True, vmem_limit_bytes=63 * 2**20
        ),
        name="banded_attention_gradients",
    )(
        query,
        dout,
        output,
        keys.reshape(flat, dm.width),
        values.reshape(flat, dm.width),
    )


def solution(mesh):
    def on_device(query, keys, values, output, dout):
        dm = Dims(query, keys, mesh)
        dquery, dkeys, dvalues = fused(dm, query, keys, values, output, dout)
        return dquery, dkeys.reshape(keys.shape), dvalues.reshape(values.shape)

    spec = P(("blk", "head"), None, None)
    return jax.shard_map(
        on_device, mesh=mesh, in_specs=(spec,) * 5, out_specs=(spec,) * 3, check_vma=False
    )
```

```python
import functools
import math

import jax
import jax.numpy as jnp
from jax import lax
from jax.experimental import pallas as pl
from jax.experimental.pallas import tpu as pltpu
from jax.sharding import PartitionSpec as P

BF = jnp.bfloat16
F32 = jnp.float32
MINOR = (((1,), (1,)), ((), ()))
MESH = pl.DeviceIdType.MESH
ANY = pl.BlockSpec(memory_space=pl.ANY)
VMEM = pl.BlockSpec(memory_space=pltpu.VMEM)


class Dims:
    def __init__(self, query, keys, mesh):
        self.tokens, self.q_heads, self.width = query.shape
        self.kv_heads = keys.shape[1]
        self.n_head = mesh.shape["head"]
        self.n_blk = mesh.shape["blk"]
        self.reach = self.n_blk // 8
        self.slots = 2 * self.reach + 1
        self.block = self.tokens * self.n_head
        self.group = self.q_heads // self.n_head
        self.chunk = self.tokens * self.group
        self.rows = self.chunk * self.n_head
        self.scaling = self.width ** (-0.5)
        self.log2_scaling = self.scaling * math.log2(math.e)
        self.score_tile = 512
        self.grad_tile = 256


def aligned(index, size):
    return pl.ds(pl.multiple_of(index * size, size), size)


def remote(src, dst, send, recv, head=None, blk=None):
    where = {}
    if head is not None:
        where["head"] = head
    if blk is not None:
        where["blk"] = blk
    return pltpu.make_async_remote_copy(
        src_ref=src, dst_ref=dst, send_sem=send, recv_sem=recv, device_id=where, device_id_type=MESH
    )


def split_heads(dm, source, staged, wide, part):
    wide[...] = source[...].astype(F32)
    for g in range(dm.n_head):
        staged[g, part] = wide[pl.ds(g, dm.tokens, stride=dm.kv_heads), :].astype(BF)


def delta_rows(dm, dout, output, rows):
    ones = jnp.ones((8, dm.width), BF)
    for g in range(dm.n_head):
        heads = slice(g * dm.group, (g + 1) * dm.group)
        product = dout[:, heads, :].astype(F32) * output[:, heads, :].astype(F32)
        product = product.reshape(dm.chunk, dm.width)
        high = product.astype(BF)
        low = (product - high.astype(F32)).astype(BF)
        total = lax.dot_general(ones, high, MINOR, preferred_element_type=F32) + lax.dot_general(
            ones, low, MINOR, preferred_element_type=F32
        )
        rows[g] = total[0:1, :].astype(BF).astype(F32)


def score_phase(dm, keys, q_t, probs, scores, tops, sums, b, chunk, count):
    block, tile = dm.block, dm.score_tile
    count = count * dm.chunk // tile
    start = chunk * (dm.chunk // tile)
    for i in range(count + 1):
        if i < count:
            columns = aligned(start + i, tile)
            scores[i % 2] = jnp.dot(keys, q_t[:, columns], preferred_element_type=F32)
        if i > 0:
            columns = aligned(start + i - 1, tile)
            x = scores[(i - 1) % 2]
            top = jnp.max(jnp.max(x.reshape(block // 8, 8, tile), axis=0), axis=0, keepdims=True)
            p = jnp.exp2((x - top) * dm.log2_scaling)
            total = jnp.sum(jnp.sum(p.reshape(block // 8, 8, tile), axis=0), axis=0, keepdims=True)
            probs[aligned(b, block), columns] = p.astype(BF)
            tops[pl.ds(b, 1), columns] = top
            sums[pl.ds(b, 1), columns] = total


def combine(dm, tops, sums, factors):
    top = tops[...]
    weight = jnp.exp2((top - jnp.max(top, axis=0, keepdims=True)) * dm.log2_scaling)
    factors[...] = weight / jnp.sum(weight * sums[...], axis=0, keepdims=True)


def gradient_phase(dm, keys_t, values, q_t, do_t, delta, probs, factors, dq_t, small, b, chunk, count):
    block, tile = dm.block, dm.grad_tile
    per_chunk = dm.chunk // tile
    count = count * per_chunk
    start = chunk * per_chunk
    rows = aligned(b, block)
    dk = jnp.zeros((dm.width, block), F32)
    dv = jnp.zeros((dm.width, block), F32)
    for i in range(count + 1):
        if i < count:
            columns = aligned(start + i, tile)
            inner = slice((i % per_chunk) * tile, (i % per_chunk + 1) * tile)
            prob_grad = jnp.dot(values, do_t[:, columns], preferred_element_type=F32)
            grad = probs[rows, columns].astype(F32) * (prob_grad - delta[chunk + i // per_chunk, :, inner])
            small[i % 2] = grad.astype(BF)
        if i > 0:
            columns = aligned(start + i - 1, tile)
            factor = factors[pl.ds(b, 1), columns]
            scaled = factor * dm.scaling
            grad = small[(i - 1) % 2]
            do_scaled = (do_t[:, columns].astype(F32) * factor).astype(BF)
            q_scaled = (q_t[:, columns].astype(F32) * scaled).astype(BF)
            dv = dv + lax.dot_general(do_scaled, probs[rows, columns], MINOR, preferred_element_type=F32)
            dk = dk + lax.dot_general(q_scaled, grad, MINOR, preferred_element_type=F32)
            dq_t[:, columns] += jnp.dot(keys_t, grad, preferred_element_type=F32) * scaled
    return dk, dv


def pick(index, choices):
    value = choices[-1]
    for at in range(len(choices) - 2, -1, -1):
        value = jnp.where(index == at, choices[at], value)
    return value


def kernel(dm, query, dout, output, keys, values, dquery, dkeys, dvalues,
           keys_v, values_v, staged, wide, drow, dout_v, output_v, q_in, do_in, delta, kv,
           keys_t, q_t, do_t, probs, scores, small, tops, sums, factors, dq_t,
           dkv, inbox, total, heads, landed, dq,
           local, s_kv, r_kv, s_q, r_q, s_do, r_do, s_de, r_de, s_dq, r_dq, s_h, r_h,
           s_own, s_rel, r_n, s_out, r_box):
    me = lax.axis_index("head")
    position = lax.axis_index("blk")
    n, w = dm.n_head, dm.reach
    pair = me // 2
    core = lax.rem(me, 2)
    mate = pair * 2 + 1 - core
    across = [(1 - pair) * 2 + core, (1 - pair) * 2 + 1 - core]
    peers = [mate] + across
    place = lax.rem(position, w)
    a = place + 1 - 2 * lax.rem(place, 2)
    b = w - 1 - place
    o = lax.rem(place + 2, w)
    has_before = position - w >= 0
    has_after = position + w < dm.n_blk
    base = position - place

    def same(d):
        return w + d - place

    def side(d):
        return lax.rem(d - place + 2 * w, 2 * w)

    def exists(slot):
        other = position - w + slot
        return (other >= 0) & (other < dm.n_blk)

    own = [
        pltpu.make_async_copy(keys, keys_v, local.at[0]),
        pltpu.make_async_copy(values, values_v, local.at[1]),
        pltpu.make_async_copy(dout, dout_v, local.at[2]),
        pltpu.make_async_copy(output, output_v, local.at[3]),
        pltpu.make_async_copy(query.at[:, aligned(me, dm.group), :], q_in.at[me], local.at[4]),
        pltpu.make_async_copy(dout.at[:, aligned(me, dm.group), :], do_in.at[me], local.at[5]),
    ]
    for copy in own:
        copy.start()
    barrier = pltpu.get_barrier_semaphore()
    for g in peers:
        pl.semaphore_signal(barrier, inc=1, device_id={"head": g}, device_id_type=MESH)
    for c in (a, b):
        pl.semaphore_signal(barrier, inc=1, device_id={"blk": base + c}, device_id_type=MESH)

    @pl.when(has_before)
    def _():
        pl.semaphore_signal(barrier, inc=1, device_id={"blk": position - w}, device_id_type=MESH)

    @pl.when(has_after)
    def _():
        pl.semaphore_signal(barrier, inc=1, device_id={"blk": position + w}, device_id_type=MESH)

    own[0].wait()
    split_heads(dm, keys_v, staged, wide, 0)
    own[1].wait()
    split_heads(dm, values_v, staged, wide, 1)
    groups = position // w
    ends = jnp.minimum(groups, 1) + jnp.minimum(dm.n_blk // w - 1 - groups, 1)
    pl.semaphore_wait(barrier, n - 1 + 2 + ends)

    def kv_copy(g, source, to):
        return remote(staged.at[g], kv.at[w, :, aligned(source, dm.tokens), :], s_kv.at[g], r_kv.at[source], head=to)

    def q_copy(g, source, to):
        return remote(query.at[:, aligned(g, dm.group), :], q_in.at[source], s_q.at[g], r_q.at[source], head=to)

    def do_copy(g, source, to):
        return remote(dout.at[:, aligned(g, dm.group), :], do_in.at[source], s_do.at[g], r_do.at[source], head=to)

    def de_copy(g, source, to):
        return remote(drow.at[g], delta.at[source], s_de.at[g], r_de.at[source], head=to)

    for make in (kv_copy, q_copy):
        for g in peers:
            make(g, me, g).start()
    kv_own = pltpu.make_async_copy(staged.at[me], kv.at[w, :, aligned(me, dm.tokens), :], local.at[6])
    kv_own.start()
    own[4].wait()

    def turn(source, target, g):
        target[:, aligned(g, dm.chunk)] = source[g].astype(F32).reshape(dm.chunk, dm.width).T.astype(BF)

    turn(q_in, q_t, me)
    kv_own.wait()
    for g in peers:
        kv_copy(me, g, g).wait_recv()

    def hop(source, slot, sem, to):
        return remote(kv.at[source], kv.at[slot], sem, r_n.at[slot], blk=to)

    def arrived(slot):
        hop(slot, slot, s_own.at[0], base + a).wait_recv()

    to_a = hop(w, w + place - a, s_own.at[0], base + a)
    to_b = hop(w, w + place - b, s_own.at[1], base + b)
    to_before = hop(w, 2 * w, s_own.at[2], position - w)
    to_after = hop(w, 0, s_own.at[3], position + w)
    on_same = hop(same(a), w + a - b, s_rel.at[0], base + b)
    before_on = [hop(0, place - d, s_rel.at[1 + k], base + d) for k, d in enumerate((a, b))]
    after_on = [hop(2 * w, 2 * w + place - d, s_rel.at[1 + k], base + d) for k, d in enumerate((a, b))]
    on_side = hop(side(b), lax.rem(b - a + 2 * w, 2 * w), s_rel.at[3], base + a)
    to_a.start()
    to_b.start()

    @pl.when(has_before)
    def _():
        to_before.start()

    @pl.when(has_after)
    def _():
        to_after.start()

    own[2].wait()
    own[3].wait()
    delta_rows(dm, dout_v, output_v, drow)
    for g in peers:
        de_copy(g, me, g).start()
    de_own = pltpu.make_async_copy(drow.at[me], delta.at[me], local.at[7])
    de_own.start()
    for at in range(0, dm.rows, 512):
        dq_t[:, at:at + 512] = jnp.zeros((dm.width, 512), F32)
    tops[...] = jnp.full((dm.slots, dm.rows), -jnp.inf, F32)
    sums[...] = jnp.zeros((dm.slots, dm.rows), F32)
    q_copy(me, mate, mate).wait_recv()
    turn(q_in, q_t, mate)

    def early(j):
        return pick(j, [jnp.int32(w), same(a), same(b), jnp.int32(0), jnp.int32(2 * w)])

    def late(j):
        return pick(j, [side(b), same(o), side(a), side(o)])

    @pl.loop(0, w + 1)
    def _(j):
        slot = early(j)

        @pl.when(exists(slot))
        def _():
            @pl.when(j > 0)
            def _():
                arrived(slot)

            @pl.when(j == 1)
            def _():
                on_same.start()

            for k, d in enumerate((a, b)):

                @pl.when((j == 3) & (d < place))
                def _():
                    before_on[k].start()

                @pl.when((j == 4) & (d > place))
                def _():
                    after_on[k].start()

            keys_t[:, aligned(slot, dm.block)] = kv[slot, 0].T
            score_phase(dm, kv[slot, 0], q_t, probs, scores, tops, sums, slot, pair * 2, 2)

    for g in peers:
        do_copy(g, me, g).start()
    for g in across:
        q_copy(me, g, g).wait_recv()
        turn(q_in, q_t, g)

    @pl.loop(0, w + 1)
    def _(j):
        slot = early(j)

        @pl.when(exists(slot))
        def _():
            score_phase(dm, kv[slot, 0], q_t, probs, scores, tops, sums, slot, (1 - pair) * 2, 2)

    own[5].wait()
    turn(do_in, do_t, me)
    de_own.wait()
    do_copy(me, mate, mate).wait_recv()
    turn(do_in, do_t, mate)

    @pl.loop(0, w)
    def _(j):
        slot = late(j)

        @pl.when(exists(slot))
        def _():
            arrived(slot)

            @pl.when(j == 0)
            def _():
                on_side.start()

            keys_t[:, aligned(slot, dm.block)] = kv[slot, 0].T
            score_phase(dm, kv[slot, 0], q_t, probs, scores, tops, sums, slot, 0, 4)

    combine(dm, tops, sums, factors)
    de_copy(me, mate, mate).wait_recv()
    for g in across:
        do_copy(me, g, g).wait_recv()
        de_copy(me, g, g).wait_recv()
        turn(do_in, do_t, g)

    def give(slot, box, k, to):
        return remote(dkv.at[slot], inbox.at[box], s_out.at[k], r_box.at[box], blk=to)

    def taken(box):
        give(w, box, box, base + a).wait_recv()

    def gradients(slot, chunk, count):
        return gradient_phase(
            dm, keys_t[:, aligned(slot, dm.block)], kv[slot, 1], q_t, do_t, delta, probs, factors, dq_t, small,
            slot, chunk, count
        )

    def first(j):
        return pick(j, [side(o), same(o), side(a), side(b), same(b)])

    def last(j):
        return pick(j, [jnp.int32(0), jnp.int32(2 * w), same(a), jnp.int32(w)])

    def add(slot, box):
        taken(box)
        dkv[slot] = (dkv[slot].astype(F32) + inbox[box].astype(F32)).astype(BF)

    @pl.loop(0, w + 1)
    def _(j):
        slot = first(j)

        @pl.when(exists(slot))
        def _():
            dk, dv = gradients(slot, 0, 4)
            dkv[slot, 0] = dk.astype(BF)
            dkv[slot, 1] = dv.astype(BF)

            @pl.when(j == 3)
            def _():
                add(slot, 0)

            give(slot, j, j, base + pick(j, [a, b, a, b, b])).start()

    @pl.loop(0, w)
    def _(j):
        slot = last(j)

        @pl.when(exists(slot))
        def _():
            dk, dv = gradients(slot, (1 - pair) * 2, 2)
            dkv[slot, 0] = dk.astype(BF)
            dkv[slot, 1] = dv.astype(BF)

    def dq_copy(g, source, to):
        return remote(dq.at[g], dquery.at[:, aligned(source, dm.group), :], s_dq.at[g], r_dq.at[source], head=to)

    def turn_back(g):
        dq[g] = dq_t[:, aligned(g, dm.chunk)].T.reshape(dm.tokens, dm.group, dm.width).astype(BF)

    for g in across:
        turn_back(g)
        dq_copy(g, me, g).start()

    @pl.loop(0, w)
    def _(j):
        slot = last(j)

        @pl.when(exists(slot))
        def _():
            dk, dv = gradients(slot, pair * 2, 2)
            dkv[slot, 0] = (dkv[slot, 0].astype(F32) + dk).astype(BF)
            dkv[slot, 1] = (dkv[slot, 1].astype(F32) + dv).astype(BF)

            @pl.when(j == 0)
            def _():
                for box, d in ((2, a), (3, b)):

                    @pl.when(d < place)
                    def _():
                        add(0, box)

                give(0, 7, 6, position - w).start()

            @pl.when(j == 1)
            def _():
                for box, d in ((2, a), (3, b)):

                    @pl.when(d > place)
                    def _():
                        add(2 * w, box)

                give(2 * w, 6, 7, position + w).start()

            @pl.when(j == 2)
            def _():
                add(same(a), 1)
                give(same(a), 5, 5, base + a).start()

    turn_back(mate)
    dq_copy(mate, me, mate).start()
    turn_back(me)
    dq_own = pltpu.make_async_copy(dq.at[me], dquery.at[:, aligned(me, dm.group), :], local.at[8])
    dq_own.start()

    total[...] = dkv[w].astype(F32)
    taken(4)
    total[...] += inbox[4].astype(F32)

    @pl.when(has_before)
    def _():
        taken(6)
        total[...] += inbox[6].astype(F32)

    @pl.when(has_after)
    def _():
        taken(7)
        total[...] += inbox[7].astype(F32)

    taken(5)
    total[...] += inbox[5].astype(F32)
    for part in range(2):
        rows = total[part].T.astype(BF)
        for g in range(n):
            heads[g, part] = rows[g * dm.tokens:(g + 1) * dm.tokens, :]

    def head_copy(g, source, to):
        return remote(heads.at[g], landed.at[source], s_h.at[g], r_h.at[source], head=to)

    for g in peers:
        head_copy(g, me, g).start()
    head_own = pltpu.make_async_copy(heads.at[me], landed.at[me], local.at[9])
    head_own.start()
    head_own.wait()
    for g in peers:
        head_copy(me, g, g).wait_recv()
    for part, out in ((0, dkeys), (1, dvalues)):
        for g in range(n):
            wide[pl.ds(g, dm.tokens, stride=dm.kv_heads), :] = landed[g, part].astype(F32)
        out[...] = wide[...].astype(BF)

    dq_own.wait()
    for g in peers:
        for make in (kv_copy, q_copy, do_copy, de_copy, dq_copy, head_copy):
            make(g, me, g).wait_send()
        dq_copy(me, g, g).wait_recv()
    to_a.wait_send()
    to_b.wait_send()
    on_same.wait_send()

    @pl.when(has_before)
    def _():
        to_before.wait_send()
        give(0, 7, 6, position - w).wait_send()

    @pl.when(has_after)
    def _():
        to_after.wait_send()
        give(2 * w, 6, 7, position + w).wait_send()

    for k, d in enumerate((a, b)):

        @pl.when((d < place) & has_before)
        def _():
            before_on[k].wait_send()

        @pl.when((d > place) & has_after)
        def _():
            after_on[k].wait_send()

    @pl.when(exists(side(b)))
    def _():
        on_side.wait_send()

    for j in range(w + 1):
        slot = [side(o), same(o), side(a), side(b), same(b)][j]

        @pl.when(exists(slot))
        def _():
            give(slot, j, j, base + [a, b, a, b, b][j]).wait_send()

    give(same(a), 5, 5, base + a).wait_send()


def fused(dm, query, keys, values, output, dout):
    n, w, dma = dm.n_head, dm.reach, pltpu.SemaphoreType.DMA
    flat = dm.tokens * dm.kv_heads
    span = dm.slots * dm.block
    chunked = (n, dm.tokens, dm.group, dm.width)
    terms = (2, dm.width, dm.block)
    return pl.pallas_call(
        functools.partial(kernel, dm),
        out_shape=(
            jax.ShapeDtypeStruct(query.shape, BF),
            jax.ShapeDtypeStruct((flat, dm.width), BF),
            jax.ShapeDtypeStruct((flat, dm.width), BF),
        ),
        in_specs=[ANY] * 5,
        out_specs=[ANY, VMEM, VMEM],
        scratch_shapes=[
            pltpu.VMEM((flat, dm.width), BF),
            pltpu.VMEM((flat, dm.width), BF),
            pltpu.VMEM((n, 2, dm.tokens, dm.width), BF),
            pltpu.VMEM((flat, dm.width), F32),
            pltpu.VMEM((n, 1, dm.chunk), F32),
            pltpu.VMEM(query.shape, BF),
            pltpu.VMEM(query.shape, BF),
            pltpu.VMEM(chunked, BF),
            pltpu.VMEM(chunked, BF),
            pltpu.VMEM((n, 1, dm.chunk), F32),
            pltpu.VMEM((dm.slots, 2, dm.block, dm.width), BF),
            pltpu.VMEM((dm.width, span), BF),
            pltpu.VMEM((dm.width, dm.rows), BF),
            pltpu.VMEM((dm.width, dm.rows), BF),
            pltpu.VMEM((span, dm.rows), BF),
            pltpu.VMEM((2, dm.block, dm.score_tile), F32),
            pltpu.VMEM((2, dm.block, dm.grad_tile), BF),
            pltpu.VMEM((dm.slots, dm.rows), F32),
            pltpu.VMEM((dm.slots, dm.rows), F32),
            pltpu.VMEM((dm.slots, dm.rows), F32),
            pltpu.VMEM((dm.width, dm.rows), F32),
            pltpu.VMEM((dm.slots,) + terms, BF),
            pltpu.VMEM((2 * w,) + terms, BF),
            pltpu.VMEM(terms, F32),
            pltpu.VMEM((n, 2, dm.tokens, dm.width), BF),
            pltpu.VMEM((n, 2, dm.tokens, dm.width), BF),
            pltpu.VMEM(chunked, BF),
            dma((10,)),
        ]
        + [dma((n,))] * 12
        + [dma((4,)), dma((4,)), dma((dm.slots,)), dma((8,)), dma((8,))],
        compiler_params=pltpu.CompilerParams(
            collective_id=0, has_side_effects=True, vmem_limit_bytes=63 * 2**20
        ),
        name="banded_attention_gradients",
    )(
        query,
        dout,
        output,
        keys.reshape(flat, dm.width),
        values.reshape(flat, dm.width),
    )


def solution(mesh):
    def on_device(query, keys, values, output, dout):
        dm = Dims(query, keys, mesh)
        dquery, dkeys, dvalues = fused(dm, query, keys, values, output, dout)
        return dquery, dkeys.reshape(keys.shape), dvalues.reshape(values.shape)

    spec = P(("blk", "head"), None, None)
    return jax.shard_map(
        on_device, mesh=mesh, in_specs=(spec,) * 5, out_specs=(spec,) * 3, check_vma=False
    )
```

```python
import functools
import math

import jax
import jax.numpy as jnp
from jax import lax
from jax.experimental import pallas as pl
from jax.experimental.pallas import tpu as pltpu
from jax.sharding import PartitionSpec as P

BF = jnp.bfloat16
F32 = jnp.float32
MINOR = (((1,), (1,)), ((), ()))
MESH = pl.DeviceIdType.MESH
ANY = pl.BlockSpec(memory_space=pl.ANY)
VMEM = pl.BlockSpec(memory_space=pltpu.VMEM)


class Dims:
    def __init__(self, query, keys, mesh):
        self.tokens, self.q_heads, self.width = query.shape
        self.kv_heads = keys.shape[1]
        self.n_head = mesh.shape["head"]
        self.n_blk = mesh.shape["blk"]
        self.reach = self.n_blk // 8
        self.slots = 2 * self.reach + 1
        self.block = self.tokens * self.n_head
        self.group = self.q_heads // self.n_head
        self.chunk = self.tokens * self.group
        self.rows = self.chunk * self.n_head
        self.scaling = self.width ** (-0.5)
        self.log2_scaling = self.scaling * math.log2(math.e)
        self.score_tile = 512
        self.grad_tile = 256


def aligned(index, size):
    return pl.ds(pl.multiple_of(index * size, size), size)


def remote(src, dst, send, recv, head=None, blk=None):
    where = {}
    if head is not None:
        where["head"] = head
    if blk is not None:
        where["blk"] = blk
    return pltpu.make_async_remote_copy(
        src_ref=src, dst_ref=dst, send_sem=send, recv_sem=recv, device_id=where, device_id_type=MESH
    )


def split_heads(dm, source, staged, wide, part):
    wide[...] = source[...].astype(F32)
    for g in range(dm.n_head):
        staged[g, part] = wide[pl.ds(g, dm.tokens, stride=dm.kv_heads), :].astype(BF)


def delta_rows(dm, dout, output, rows):
    ones = jnp.ones((8, dm.width), BF)
    for g in range(dm.n_head):
        heads = slice(g * dm.group, (g + 1) * dm.group)
        product = dout[:, heads, :].astype(F32) * output[:, heads, :].astype(F32)
        product = product.reshape(dm.chunk, dm.width)
        high = product.astype(BF)
        low = (product - high.astype(F32)).astype(BF)
        total = lax.dot_general(ones, high, MINOR, preferred_element_type=F32) + lax.dot_general(
            ones, low, MINOR, preferred_element_type=F32
        )
        rows[g] = total[0:1, :].astype(BF).astype(F32)


def score_phase(dm, keys, q_t, probs, scores, tops, sums, b, chunk, count):
    block, tile = dm.block, dm.score_tile
    count = count * dm.chunk // tile
    start = chunk * (dm.chunk // tile)
    for i in range(count + 1):
        if i < count:
            columns = aligned(start + i, tile)
            scores[i % 2] = jnp.dot(keys, q_t[:, columns], preferred_element_type=F32)
        if i > 0:
            columns = aligned(start + i - 1, tile)
            x = scores[(i - 1) % 2]
            top = jnp.max(jnp.max(x.reshape(block // 8, 8, tile), axis=0), axis=0, keepdims=True)
            p = jnp.exp2((x - top) * dm.log2_scaling)
            total = jnp.sum(jnp.sum(p.reshape(block // 8, 8, tile), axis=0), axis=0, keepdims=True)
            probs[aligned(b, block), columns] = p.astype(BF)
            tops[pl.ds(b, 1), columns] = top
            sums[pl.ds(b, 1), columns] = total


def combine(dm, tops, sums, factors):
    top = tops[...]
    weight = jnp.exp2((top - jnp.max(top, axis=0, keepdims=True)) * dm.log2_scaling)
    factors[...] = weight / jnp.sum(weight * sums[...], axis=0, keepdims=True)


def gradient_phase(dm, keys_t, values, q_t, do_t, delta, probs, factors, dq_t, small, b, chunk, count):
    block, tile = dm.block, dm.grad_tile
    per_chunk = dm.chunk // tile
    count = count * per_chunk
    start = chunk * per_chunk
    rows = aligned(b, block)
    dk = jnp.zeros((dm.width, block), F32)
    dv = jnp.zeros((dm.width, block), F32)
    for i in range(count + 1):
        if i < count:
            columns = aligned(start + i, tile)
            inner = slice((i % per_chunk) * tile, (i % per_chunk + 1) * tile)
            prob_grad = jnp.dot(values, do_t[:, columns], preferred_element_type=F32)
            grad = probs[rows, columns].astype(F32) * (prob_grad - delta[chunk + i // per_chunk, :, inner])
            small[i % 2] = grad.astype(BF)
        if i > 0:
            columns = aligned(start + i - 1, tile)
            factor = factors[pl.ds(b, 1), columns]
            scaled = factor * dm.scaling
            grad = small[(i - 1) % 2]
            do_scaled = (do_t[:, columns].astype(F32) * factor).astype(BF)
            q_scaled = (q_t[:, columns].astype(F32) * scaled).astype(BF)
            dv = dv + lax.dot_general(do_scaled, probs[rows, columns], MINOR, preferred_element_type=F32)
            dk = dk + lax.dot_general(q_scaled, grad, MINOR, preferred_element_type=F32)
            dq_t[:, columns] += jnp.dot(keys_t, grad, preferred_element_type=F32) * scaled
    return dk, dv


def pick(index, choices):
    value = choices[-1]
    for at in range(len(choices) - 2, -1, -1):
        value = jnp.where(index == at, choices[at], value)
    return value


def kernel(dm, query, dout, output, keys, values, dquery, dkeys, dvalues,
           keys_v, values_v, staged, wide, drow, dout_v, output_v, q_in, do_in, delta, kv,
           keys_t, q_t, do_t, probs, scores, small, tops, sums, factors, dq_t,
           dkv, inbox, total, heads, landed, dq,
           local, s_kv, r_kv, s_q, r_q, s_do, r_do, s_de, r_de, s_dq, r_dq, s_h, r_h,
           s_hop, r_n, s_out, r_box):
    me = lax.axis_index("head")
    position = lax.axis_index("blk")
    n, w = dm.n_head, dm.reach
    pair = me // 2
    core = lax.rem(me, 2)
    mate = pair * 2 + 1 - core
    across = [(1 - pair) * 2 + core, (1 - pair) * 2 + 1 - core]
    peers = [mate] + across
    place = lax.rem(position, w)
    a = place + 1 - 2 * lax.rem(place, 2)
    b = w - 1 - place
    o = lax.rem(place + 2, w)
    has_before = position - w >= 0
    has_after = position + w < dm.n_blk
    base = position - place

    def same(d):
        return w + d - place

    def side(d):
        return lax.rem(d - place + 2 * w, 2 * w)

    def exists(slot):
        other = position - w + slot
        return (other >= 0) & (other < dm.n_blk)

    own = [
        pltpu.make_async_copy(keys, keys_v, local.at[0]),
        pltpu.make_async_copy(values, values_v, local.at[1]),
        pltpu.make_async_copy(dout, dout_v, local.at[2]),
        pltpu.make_async_copy(output, output_v, local.at[3]),
        pltpu.make_async_copy(query.at[:, aligned(me, dm.group), :], q_in.at[me], local.at[4]),
        pltpu.make_async_copy(dout.at[:, aligned(me, dm.group), :], do_in.at[me], local.at[5]),
    ]
    for copy in own:
        copy.start()
    barrier = pltpu.get_barrier_semaphore()
    for g in peers:
        pl.semaphore_signal(barrier, inc=1, device_id={"head": g}, device_id_type=MESH)
    for c in (a, b):
        pl.semaphore_signal(barrier, inc=1, device_id={"blk": base + c}, device_id_type=MESH)

    @pl.when(has_before)
    def _():
        pl.semaphore_signal(barrier, inc=1, device_id={"blk": position - w}, device_id_type=MESH)

    @pl.when(has_after)
    def _():
        pl.semaphore_signal(barrier, inc=1, device_id={"blk": position + w}, device_id_type=MESH)

    own[0].wait()
    split_heads(dm, keys_v, staged, wide, 0)
    groups = position // w
    ends = jnp.minimum(groups, 1) + jnp.minimum(dm.n_blk // w - 1 - groups, 1)
    pl.semaphore_wait(barrier, n - 1 + 2 + ends)

    def part_copy(part, g, source, to):
        return remote(staged.at[g, part], kv.at[w, part, aligned(source, dm.tokens), :],
                      s_kv.at[part, g], r_kv.at[part, source], head=to)

    def k_copy(g, source, to):
        return part_copy(0, g, source, to)

    def v_copy(g, source, to):
        return part_copy(1, g, source, to)

    def q_copy(g, source, to):
        return remote(query.at[:, aligned(g, dm.group), :], q_in.at[source], s_q.at[g], r_q.at[source], head=to)

    def do_copy(g, source, to):
        return remote(dout.at[:, aligned(g, dm.group), :], do_in.at[source], s_do.at[g], r_do.at[source], head=to)

    def de_copy(g, source, to):
        return remote(drow.at[g], delta.at[source], s_de.at[g], r_de.at[source], head=to)

    for g in peers:
        k_copy(g, me, g).start()
    k_own = pltpu.make_async_copy(staged.at[me, 0], kv.at[w, 0, aligned(me, dm.tokens), :], local.at[6])
    k_own.start()
    for g in peers:
        q_copy(g, me, g).start()
    own[1].wait()
    split_heads(dm, values_v, staged, wide, 1)
    for g in peers:
        v_copy(g, me, g).start()
    v_own = pltpu.make_async_copy(staged.at[me, 1], kv.at[w, 1, aligned(me, dm.tokens), :], local.at[10])
    v_own.start()
    own[4].wait()

    def turn(source, target, g):
        target[:, aligned(g, dm.chunk)] = source[g].astype(F32).reshape(dm.chunk, dm.width).T.astype(BF)

    turn(q_in, q_t, me)
    k_own.wait()
    for g in peers:
        k_copy(me, g, g).wait_recv()

    def hop(part, source, slot, k, to):
        return remote(kv.at[source, part], kv.at[slot, part], s_hop.at[part, k], r_n.at[part, slot], blk=to)

    def arrived(part, slot):
        hop(part, slot, slot, 0, base + a).wait_recv()

    def from_own(part, act):
        act(hop(part, w, w + place - a, 0, base + a))
        act(hop(part, w, w + place - b, 1, base + b))

        @pl.when(has_before)
        def _():
            act(hop(part, w, 2 * w, 2, position - w))

        @pl.when(has_after)
        def _():
            act(hop(part, w, 0, 3, position + w))

    def from_first(part, act):
        for k, d in enumerate((a, b)):

            @pl.when(has_before & (d < place))
            def _():
                act(hop(part, 0, place - d, 4 + k, base + d))

            @pl.when(has_after & (d > place))
            def _():
                act(hop(part, 2 * w, 2 * w + place - d, 4 + k, base + d))

        act(hop(part, same(a), w + a - b, 6, base + b))

    def from_second(part, act):
        @pl.when(exists(side(b)))
        def _():
            act(hop(part, side(b), lax.rem(b - a + 2 * w, 2 * w), 7, base + a))

    def pass_first(part):
        @pl.when(has_before)
        def _():
            arrived(part, 0)

        @pl.when(has_after)
        def _():
            arrived(part, 2 * w)

        arrived(part, same(a))
        from_first(part, lambda copy: copy.start())

    def pass_second(part):
        @pl.when(exists(side(b)))
        def _():
            arrived(part, side(b))

        from_second(part, lambda copy: copy.start())

    from_own(0, lambda copy: copy.start())
    own[2].wait()
    own[3].wait()
    delta_rows(dm, dout_v, output_v, drow)
    for g in peers:
        de_copy(g, me, g).start()
    de_own = pltpu.make_async_copy(drow.at[me], delta.at[me], local.at[7])
    de_own.start()
    for at in range(0, dm.rows, 512):
        dq_t[:, at:at + 512] = jnp.zeros((dm.width, 512), F32)
    tops[...] = jnp.full((dm.slots, dm.rows), -jnp.inf, F32)
    sums[...] = jnp.zeros((dm.slots, dm.rows), F32)
    q_copy(me, mate, mate).wait_recv()
    turn(q_in, q_t, mate)

    def order(j):
        return pick(j, [jnp.int32(w), same(a), same(b), jnp.int32(0), jnp.int32(2 * w),
                        side(b), side(a), same(o), side(o)])

    @pl.loop(0, dm.slots)
    def _(j):
        slot = order(j)

        @pl.when(j == 1)
        def _():
            pass_first(0)
            arrived(0, same(b))
            v_own.wait()
            for g in peers:
                v_copy(me, g, g).wait_recv()
            from_own(1, lambda copy: copy.start())

        @pl.when(j == 5)
        def _():
            pass_second(0)
            for g in peers:
                do_copy(g, me, g).start()

        @pl.when(j == 7)
        def _():
            pass_first(1)

        @pl.when(exists(slot))
        def _():
            @pl.when(j > 5)
            def _():
                arrived(0, slot)

            keys_t[:, aligned(slot, dm.block)] = kv[slot, 0].T
            score_phase(dm, kv[slot, 0], q_t, probs, scores, tops, sums, slot, pair * 2, 2)

    for g in across:
        q_copy(me, g, g).wait_recv()
        turn(q_in, q_t, g)

    @pl.loop(0, dm.slots)
    def _(j):
        slot = order(j)

        @pl.when(j == 5)
        def _():
            pass_second(1)

        @pl.when(exists(slot))
        def _():
            score_phase(dm, kv[slot, 0], q_t, probs, scores, tops, sums, slot, (1 - pair) * 2, 2)

    combine(dm, tops, sums, factors)
    own[5].wait()
    turn(do_in, do_t, me)
    de_own.wait()
    for g in [mate] + across:
        do_copy(me, g, g).wait_recv()
        de_copy(me, g, g).wait_recv()
        turn(do_in, do_t, g)
    arrived(1, same(b))
    arrived(1, same(o))
    for d in (a, o):

        @pl.when(exists(side(d)))
        def _():
            arrived(1, side(d))

    def give(slot, box, k, to):
        return remote(dkv.at[slot], inbox.at[box], s_out.at[k], r_box.at[box], blk=to)

    def taken(box):
        give(w, box, box, base + a).wait_recv()

    def gradients(slot, chunk, count):
        return gradient_phase(
            dm, keys_t[:, aligned(slot, dm.block)], kv[slot, 1], q_t, do_t, delta, probs, factors, dq_t, small,
            slot, chunk, count
        )

    def first(j):
        return pick(j, [side(o), same(o), side(a)])

    def last(j):
        return pick(j, [side(b), same(a), same(b), jnp.int32(0), jnp.int32(2 * w), jnp.int32(w)])

    def add(slot, box):
        taken(box)
        dkv[slot] = (dkv[slot].astype(F32) + inbox[box].astype(F32)).astype(BF)

    @pl.loop(0, 3)
    def _(j):
        slot = first(j)

        @pl.when(exists(slot))
        def _():
            dk, dv = gradients(slot, 0, 4)
            dkv[slot, 0] = dk.astype(BF)
            dkv[slot, 1] = dv.astype(BF)
            give(slot, j, j, base + pick(j, [a, b, a])).start()

    @pl.loop(0, 6)
    def _(j):
        slot = last(j)

        @pl.when(exists(slot))
        def _():
            dk, dv = gradients(slot, (1 - pair) * 2, 2)
            dkv[slot, 0] = dk.astype(BF)
            dkv[slot, 1] = dv.astype(BF)

    def dq_copy(g, source, to):
        return remote(dq.at[g], dquery.at[:, aligned(source, dm.group), :], s_dq.at[g], r_dq.at[source], head=to)

    def turn_back(g):
        dq[g] = dq_t[:, aligned(g, dm.chunk)].T.reshape(dm.tokens, dm.group, dm.width).astype(BF)

    for g in across:
        turn_back(g)
        dq_copy(g, me, g).start()

    @pl.loop(0, 6)
    def _(j):
        slot = last(j)

        @pl.when(exists(slot))
        def _():
            dk, dv = gradients(slot, pair * 2, 2)
            dkv[slot, 0] = (dkv[slot, 0].astype(F32) + dk).astype(BF)
            dkv[slot, 1] = (dkv[slot, 1].astype(F32) + dv).astype(BF)

            @pl.when(j == 0)
            def _():
                add(slot, 0)
                give(slot, 3, 3, base + b).start()

            @pl.when(j == 1)
            def _():
                add(slot, 1)
                give(slot, 5, 5, base + a).start()

            @pl.when(j == 2)
            def _():
                give(slot, 4, 4, base + b).start()

            @pl.when(j == 3)
            def _():
                for box, d in ((2, a), (3, b)):

                    @pl.when(d < place)
                    def _():
                        add(0, box)

                give(0, 7, 6, position - w).start()

            @pl.when(j == 4)
            def _():
                for box, d in ((2, a), (3, b)):

                    @pl.when(d > place)
                    def _():
                        add(2 * w, box)

                give(2 * w, 6, 7, position + w).start()

    turn_back(mate)
    dq_copy(mate, me, mate).start()
    turn_back(me)
    dq_own = pltpu.make_async_copy(dq.at[me], dquery.at[:, aligned(me, dm.group), :], local.at[8])
    dq_own.start()

    total[...] = dkv[w].astype(F32)
    for box in (5, 4):
        taken(box)
        total[...] += inbox[box].astype(F32)

    @pl.when(has_before)
    def _():
        taken(6)
        total[...] += inbox[6].astype(F32)

    @pl.when(has_after)
    def _():
        taken(7)
        total[...] += inbox[7].astype(F32)

    for part in range(2):
        rows = total[part].T.astype(BF)
        for g in range(n):
            heads[g, part] = rows[g * dm.tokens:(g + 1) * dm.tokens, :]

    def head_copy(g, source, to):
        return remote(heads.at[g], landed.at[source], s_h.at[g], r_h.at[source], head=to)

    for g in peers:
        head_copy(g, me, g).start()
    head_own = pltpu.make_async_copy(heads.at[me], landed.at[me], local.at[9])
    head_own.start()
    head_own.wait()
    for g in peers:
        head_copy(me, g, g).wait_recv()
    for part, out in ((0, dkeys), (1, dvalues)):
        for g in range(n):
            wide[pl.ds(g, dm.tokens, stride=dm.kv_heads), :] = landed[g, part].astype(F32)
        out[...] = wide[...].astype(BF)

    dq_own.wait()
    for g in peers:
        for make in (k_copy, v_copy, q_copy, do_copy, de_copy, dq_copy, head_copy):
            make(g, me, g).wait_send()
        dq_copy(me, g, g).wait_recv()
    for part in range(2):
        for group in (from_own, from_first, from_second):
            group(part, lambda copy: copy.wait_send())

    @pl.when(has_before)
    def _():
        give(0, 7, 6, position - w).wait_send()

    @pl.when(has_after)
    def _():
        give(2 * w, 6, 7, position + w).wait_send()

    for j in range(w + 1):
        slot = [side(o), same(o), side(a), side(b), same(b)][j]

        @pl.when(exists(slot))
        def _():
            give(slot, j, j, base + [a, b, a, b, b][j]).wait_send()

    give(same(a), 5, 5, base + a).wait_send()


def fused(dm, query, keys, values, output, dout):
    n, w, dma = dm.n_head, dm.reach, pltpu.SemaphoreType.DMA
    flat = dm.tokens * dm.kv_heads
    span = dm.slots * dm.block
    chunked = (n, dm.tokens, dm.group, dm.width)
    terms = (2, dm.width, dm.block)
    return pl.pallas_call(
        functools.partial(kernel, dm),
        out_shape=(
            jax.ShapeDtypeStruct(query.shape, BF),
            jax.ShapeDtypeStruct((flat, dm.width), BF),
            jax.ShapeDtypeStruct((flat, dm.width), BF),
        ),
        in_specs=[ANY] * 5,
        out_specs=[ANY, VMEM, VMEM],
        scratch_shapes=[
            pltpu.VMEM((flat, dm.width), BF),
            pltpu.VMEM((flat, dm.width), BF),
            pltpu.VMEM((n, 2, dm.tokens, dm.width), BF),
            pltpu.VMEM((flat, dm.width), F32),
            pltpu.VMEM((n, 1, dm.chunk), F32),
            pltpu.VMEM(query.shape, BF),
            pltpu.VMEM(query.shape, BF),
            pltpu.VMEM(chunked, BF),
            pltpu.VMEM(chunked, BF),
            pltpu.VMEM((n, 1, dm.chunk), F32),
            pltpu.VMEM((dm.slots, 2, dm.block, dm.width), BF),
            pltpu.VMEM((dm.width, span), BF),
            pltpu.VMEM((dm.width, dm.rows), BF),
            pltpu.VMEM((dm.width, dm.rows), BF),
            pltpu.VMEM((span, dm.rows), BF),
            pltpu.VMEM((2, dm.block, dm.score_tile), F32),
            pltpu.VMEM((2, dm.block, dm.grad_tile), BF),
            pltpu.VMEM((dm.slots, dm.rows), F32),
            pltpu.VMEM((dm.slots, dm.rows), F32),
            pltpu.VMEM((dm.slots, dm.rows), F32),
            pltpu.VMEM((dm.width, dm.rows), F32),
            pltpu.VMEM((dm.slots,) + terms, BF),
            pltpu.VMEM((2 * w,) + terms, BF),
            pltpu.VMEM(terms, F32),
            pltpu.VMEM((n, 2, dm.tokens, dm.width), BF),
            pltpu.VMEM((n, 2, dm.tokens, dm.width), BF),
            pltpu.VMEM(chunked, BF),
            dma((11,)),
        ]
        + [dma((2, n))] * 2
        + [dma((n,))] * 10
        + [dma((2, 8)), dma((2, dm.slots)), dma((8,)), dma((8,))],
        compiler_params=pltpu.CompilerParams(
            collective_id=0, has_side_effects=True, vmem_limit_bytes=63 * 2**20
        ),
        name="banded_attention_gradients",
    )(
        query,
        dout,
        output,
        keys.reshape(flat, dm.width),
        values.reshape(flat, dm.width),
    )


def solution(mesh):
    def on_device(query, keys, values, output, dout):
        dm = Dims(query, keys, mesh)
        dquery, dkeys, dvalues = fused(dm, query, keys, values, output, dout)
        return dquery, dkeys.reshape(keys.shape), dvalues.reshape(values.shape)

    spec = P(("blk", "head"), None, None)
    return jax.shard_map(
        on_device, mesh=mesh, in_specs=(spec,) * 5, out_specs=(spec,) * 3, check_vma=False
    )
```

```python
import functools
import math

import jax
import jax.numpy as jnp
from jax import lax
from jax.experimental import pallas as pl
from jax.experimental.pallas import tpu as pltpu
from jax.sharding import PartitionSpec as P

BF = jnp.bfloat16
F32 = jnp.float32
MINOR = (((1,), (1,)), ((), ()))
MESH = pl.DeviceIdType.MESH
ANY = pl.BlockSpec(memory_space=pl.ANY)
VMEM = pl.BlockSpec(memory_space=pltpu.VMEM)


class Dims:
    def __init__(self, query, keys, mesh):
        self.tokens, self.q_heads, self.width = query.shape
        self.kv_heads = keys.shape[1]
        self.n_head = mesh.shape["head"]
        self.n_blk = mesh.shape["blk"]
        self.reach = self.n_blk // 8
        self.slots = 2 * self.reach + 1
        self.block = self.tokens * self.n_head
        self.group = self.q_heads // self.n_head
        self.chunk = self.tokens * self.group
        self.rows = self.chunk * self.n_head
        self.scaling = self.width ** (-0.5)
        self.log2_scaling = self.scaling * math.log2(math.e)
        self.score_tile = 512
        self.grad_tile = 256


def aligned(index, size):
    return pl.ds(pl.multiple_of(index * size, size), size)


def remote(src, dst, send, recv, head=None, blk=None):
    where = {}
    if head is not None:
        where["head"] = head
    if blk is not None:
        where["blk"] = blk
    return pltpu.make_async_remote_copy(
        src_ref=src, dst_ref=dst, send_sem=send, recv_sem=recv, device_id=where, device_id_type=MESH
    )


def split_heads(dm, source, staged, wide, part):
    wide[...] = source[...].astype(F32)
    for g in range(dm.n_head):
        staged[g, part] = wide[pl.ds(g, dm.tokens, stride=dm.kv_heads), :].astype(BF)


def delta_rows(dm, dout, output, rows):
    ones = jnp.ones((8, dm.width), BF)
    for g in range(dm.n_head):
        heads = slice(g * dm.group, (g + 1) * dm.group)
        product = dout[:, heads, :].astype(F32) * output[:, heads, :].astype(F32)
        product = product.reshape(dm.chunk, dm.width)
        high = product.astype(BF)
        low = (product - high.astype(F32)).astype(BF)
        total = lax.dot_general(ones, high, MINOR, preferred_element_type=F32) + lax.dot_general(
            ones, low, MINOR, preferred_element_type=F32
        )
        rows[g] = total[0:1, :].astype(BF).astype(F32)


def score_phase(dm, keys, q_t, probs, scores, tops, sums, b, chunk, count):
    block, tile = dm.block, dm.score_tile
    count = count * dm.chunk // tile
    start = chunk * (dm.chunk // tile)
    for i in range(count + 1):
        if i < count:
            columns = aligned(start + i, tile)
            scores[i % 2] = jnp.dot(keys, q_t[:, columns], preferred_element_type=F32)
        if i > 0:
            columns = aligned(start + i - 1, tile)
            x = scores[(i - 1) % 2]
            top = jnp.max(jnp.max(x.reshape(block // 8, 8, tile), axis=0), axis=0, keepdims=True)
            p = jnp.exp2((x - top) * dm.log2_scaling)
            total = jnp.sum(jnp.sum(p.reshape(block // 8, 8, tile), axis=0), axis=0, keepdims=True)
            probs[aligned(b, block), columns] = p.astype(BF)
            tops[pl.ds(b, 1), columns] = top
            sums[pl.ds(b, 1), columns] = total


def combine(dm, tops, sums, factors):
    top = tops[...]
    weight = jnp.exp2((top - jnp.max(top, axis=0, keepdims=True)) * dm.log2_scaling)
    factors[...] = weight / jnp.sum(weight * sums[...], axis=0, keepdims=True)


def gradient_phase(dm, keys_t, values, q_t, do_t, delta, probs, factors, dq_t, small, b, chunk, count):
    block, tile = dm.block, dm.grad_tile
    per_chunk = dm.chunk // tile
    count = count * per_chunk
    start = chunk * per_chunk
    rows = aligned(b, block)
    dk = jnp.zeros((dm.width, block), F32)
    dv = jnp.zeros((dm.width, block), F32)
    for i in range(count + 1):
        if i < count:
            columns = aligned(start + i, tile)
            inner = slice((i % per_chunk) * tile, (i % per_chunk + 1) * tile)
            prob_grad = jnp.dot(values, do_t[:, columns], preferred_element_type=F32)
            grad = probs[rows, columns].astype(F32) * (prob_grad - delta[chunk + i // per_chunk, :, inner])
            small[i % 2] = grad.astype(BF)
        if i > 0:
            columns = aligned(start + i - 1, tile)
            factor = factors[pl.ds(b, 1), columns]
            scaled = factor * dm.scaling
            grad = small[(i - 1) % 2]
            do_scaled = (do_t[:, columns].astype(F32) * factor).astype(BF)
            q_scaled = (q_t[:, columns].astype(F32) * scaled).astype(BF)
            dv = dv + lax.dot_general(do_scaled, probs[rows, columns], MINOR, preferred_element_type=F32)
            dk = dk + lax.dot_general(q_scaled, grad, MINOR, preferred_element_type=F32)
            dq_t[:, columns] += jnp.dot(keys_t, grad, preferred_element_type=F32) * scaled
    return dk, dv


def pick(index, choices):
    value = choices[-1]
    for at in range(len(choices) - 2, -1, -1):
        value = jnp.where(index == at, choices[at], value)
    return value


def kernel(dm, query, dout, output, keys, values, dquery, dkeys, dvalues,
           keys_v, values_v, staged, wide, drow, dout_v, output_v, q_in, do_in, delta, kv,
           keys_t, q_t, do_t, probs, scores, small, tops, sums, factors, dq_t,
           dkv, inbox, total, heads, landed, dq,
           local, s_kv, r_kv, s_q, r_q, s_do, r_do, s_de, r_de, s_dq, r_dq, s_h, r_h,
           s_hop, r_n, s_out, r_box):
    me = lax.axis_index("head")
    position = lax.axis_index("blk")
    n, w = dm.n_head, dm.reach
    pair = me // 2
    core = lax.rem(me, 2)
    mate = pair * 2 + 1 - core
    across = [(1 - pair) * 2 + core, (1 - pair) * 2 + 1 - core]
    peers = [mate] + across
    place = lax.rem(position, w)
    a = place + 1 - 2 * lax.rem(place, 2)
    b = w - 1 - place
    o = lax.rem(place + 2, w)
    has_before = position - w >= 0
    has_after = position + w < dm.n_blk
    base = position - place

    def same(d):
        return w + d - place

    def side(d):
        return lax.rem(d - place + 2 * w, 2 * w)

    def exists(slot):
        other = position - w + slot
        return (other >= 0) & (other < dm.n_blk)

    own = [
        pltpu.make_async_copy(keys, keys_v, local.at[0]),
        pltpu.make_async_copy(values, values_v, local.at[1]),
        pltpu.make_async_copy(dout, dout_v, local.at[2]),
        pltpu.make_async_copy(output, output_v, local.at[3]),
        pltpu.make_async_copy(query.at[:, aligned(me, dm.group), :], q_in.at[me], local.at[4]),
        pltpu.make_async_copy(dout.at[:, aligned(me, dm.group), :], do_in.at[me], local.at[5]),
    ]
    for copy in own:
        copy.start()
    barrier = pltpu.get_barrier_semaphore()
    for g in peers:
        pl.semaphore_signal(barrier, inc=1, device_id={"head": g}, device_id_type=MESH)
    for c in (a, b):
        pl.semaphore_signal(barrier, inc=1, device_id={"blk": base + c}, device_id_type=MESH)

    @pl.when(has_before)
    def _():
        pl.semaphore_signal(barrier, inc=1, device_id={"blk": position - w}, device_id_type=MESH)

    @pl.when(has_after)
    def _():
        pl.semaphore_signal(barrier, inc=1, device_id={"blk": position + w}, device_id_type=MESH)

    own[0].wait()
    split_heads(dm, keys_v, staged, wide, 0)
    groups = position // w
    ends = jnp.minimum(groups, 1) + jnp.minimum(dm.n_blk // w - 1 - groups, 1)
    pl.semaphore_wait(barrier, n - 1 + 2 + ends)

    def part_copy(part, g, source, to):
        return remote(staged.at[g, part], kv.at[w, part, aligned(source, dm.tokens), :],
                      s_kv.at[part, g], r_kv.at[part, source], head=to)

    def k_copy(g, source, to):
        return part_copy(0, g, source, to)

    def v_copy(g, source, to):
        return part_copy(1, g, source, to)

    def q_copy(g, source, to):
        return remote(query.at[:, aligned(g, dm.group), :], q_in.at[source], s_q.at[g], r_q.at[source], head=to)

    def do_copy(g, source, to):
        return remote(dout.at[:, aligned(g, dm.group), :], do_in.at[source], s_do.at[g], r_do.at[source], head=to)

    def de_copy(g, source, to):
        return remote(drow.at[g], delta.at[source], s_de.at[g], r_de.at[source], head=to)

    for g in peers:
        k_copy(g, me, g).start()
    k_own = pltpu.make_async_copy(staged.at[me, 0], kv.at[w, 0, aligned(me, dm.tokens), :], local.at[6])
    k_own.start()
    q_copy(mate, me, mate).start()
    own[1].wait()
    split_heads(dm, values_v, staged, wide, 1)
    for g in peers:
        v_copy(g, me, g).start()
    v_own = pltpu.make_async_copy(staged.at[me, 1], kv.at[w, 1, aligned(me, dm.tokens), :], local.at[10])
    v_own.start()
    own[4].wait()

    def turn(source, target, g):
        target[:, aligned(g, dm.chunk)] = source[g].astype(F32).reshape(dm.chunk, dm.width).T.astype(BF)

    turn(q_in, q_t, me)
    k_own.wait()
    for g in peers:
        k_copy(me, g, g).wait_recv()

    def hop(part, source, slot, k, to):
        return remote(kv.at[source, part], kv.at[slot, part], s_hop.at[part, k], r_n.at[part, slot], blk=to)

    def arrived(part, slot):
        hop(part, slot, slot, 0, base + a).wait_recv()

    def from_own(part, act):
        act(hop(part, w, w + place - a, 0, base + a))
        act(hop(part, w, w + place - b, 1, base + b))

        @pl.when(has_before)
        def _():
            act(hop(part, w, 2 * w, 2, position - w))

        @pl.when(has_after)
        def _():
            act(hop(part, w, 0, 3, position + w))

    def from_first(part, act):
        for k, d in enumerate((a, b)):

            @pl.when(has_before & (d < place))
            def _():
                act(hop(part, 0, place - d, 4 + k, base + d))

            @pl.when(has_after & (d > place))
            def _():
                act(hop(part, 2 * w, 2 * w + place - d, 4 + k, base + d))

        act(hop(part, same(a), w + a - b, 6, base + b))

    def from_second(part, act):
        @pl.when(exists(side(b)))
        def _():
            act(hop(part, side(b), lax.rem(b - a + 2 * w, 2 * w), 7, base + a))

    def pass_first(part):
        @pl.when(has_before)
        def _():
            arrived(part, 0)

        @pl.when(has_after)
        def _():
            arrived(part, 2 * w)

        arrived(part, same(a))
        from_first(part, lambda copy: copy.start())

    def pass_second(part):
        @pl.when(exists(side(b)))
        def _():
            arrived(part, side(b))

        from_second(part, lambda copy: copy.start())

    from_own(0, lambda copy: copy.start())
    for g in across:
        q_copy(g, me, g).start()
    own[2].wait()
    own[3].wait()
    delta_rows(dm, dout_v, output_v, drow)
    for g in peers:
        de_copy(g, me, g).start()
    de_own = pltpu.make_async_copy(drow.at[me], delta.at[me], local.at[7])
    de_own.start()
    for at in range(0, dm.rows, 512):
        dq_t[:, at:at + 512] = jnp.zeros((dm.width, 512), F32)
    tops[...] = jnp.full((dm.slots, dm.rows), -jnp.inf, F32)
    sums[...] = jnp.zeros((dm.slots, dm.rows), F32)
    q_copy(me, mate, mate).wait_recv()
    turn(q_in, q_t, mate)

    def order(j):
        return pick(j, [jnp.int32(w), same(a), same(b), jnp.int32(0), jnp.int32(2 * w),
                        side(b), side(a), same(o), side(o)])

    @pl.loop(0, dm.slots)
    def _(j):
        slot = order(j)

        @pl.when(j == 1)
        def _():
            pass_first(0)
            arrived(0, same(b))
            v_own.wait()
            for g in peers:
                v_copy(me, g, g).wait_recv()
            from_own(1, lambda copy: copy.start())

        @pl.when(j == 5)
        def _():
            pass_second(0)

        @pl.when(j == 7)
        def _():
            pass_first(1)

        @pl.when(exists(slot))
        def _():
            @pl.when(j > 5)
            def _():
                arrived(0, slot)

            keys_t[:, aligned(slot, dm.block)] = kv[slot, 0].T
            score_phase(dm, kv[slot, 0], q_t, probs, scores, tops, sums, slot, pair * 2, 2)

    for g in across:
        q_copy(me, g, g).wait_recv()
    for g in across + [mate]:
        do_copy(g, me, g).start()
    for g in across:
        turn(q_in, q_t, g)

    @pl.loop(0, dm.slots)
    def _(j):
        slot = order(j)

        @pl.when(j == 5)
        def _():
            pass_second(1)

        @pl.when(exists(slot))
        def _():
            score_phase(dm, kv[slot, 0], q_t, probs, scores, tops, sums, slot, (1 - pair) * 2, 2)

    combine(dm, tops, sums, factors)
    own[5].wait()
    turn(do_in, do_t, me)
    de_own.wait()
    for g in [mate] + across:
        do_copy(me, g, g).wait_recv()
        de_copy(me, g, g).wait_recv()
        turn(do_in, do_t, g)
    arrived(1, same(b))
    arrived(1, same(o))
    for d in (a, o):

        @pl.when(exists(side(d)))
        def _():
            arrived(1, side(d))

    def give(slot, box, k, to):
        return remote(dkv.at[slot], inbox.at[box], s_out.at[k], r_box.at[box], blk=to)

    def taken(box):
        give(w, box, box, base + a).wait_recv()

    def gradients(slot, chunk, count):
        return gradient_phase(
            dm, keys_t[:, aligned(slot, dm.block)], kv[slot, 1], q_t, do_t, delta, probs, factors, dq_t, small,
            slot, chunk, count
        )

    def first(j):
        return pick(j, [side(o), same(o), side(a)])

    def last(j):
        return pick(j, [side(b), same(a), same(b), jnp.int32(0), jnp.int32(2 * w), jnp.int32(w)])

    def add(slot, box):
        taken(box)
        dkv[slot] = (dkv[slot].astype(F32) + inbox[box].astype(F32)).astype(BF)

    @pl.loop(0, 3)
    def _(j):
        slot = first(j)

        @pl.when(exists(slot))
        def _():
            dk, dv = gradients(slot, 0, 4)
            dkv[slot, 0] = dk.astype(BF)
            dkv[slot, 1] = dv.astype(BF)
            give(slot, j, j, base + pick(j, [a, b, a])).start()

    @pl.loop(0, 6)
    def _(j):
        slot = last(j)

        @pl.when(exists(slot))
        def _():
            dk, dv = gradients(slot, (1 - pair) * 2, 2)
            dkv[slot, 0] = dk.astype(BF)
            dkv[slot, 1] = dv.astype(BF)

    def dq_copy(g, source, to):
        return remote(dq.at[g], dquery.at[:, aligned(source, dm.group), :], s_dq.at[g], r_dq.at[source], head=to)

    def turn_back(g):
        dq[g] = dq_t[:, aligned(g, dm.chunk)].T.reshape(dm.tokens, dm.group, dm.width).astype(BF)

    for g in across:
        turn_back(g)
        dq_copy(g, me, g).start()

    @pl.loop(0, 6)
    def _(j):
        slot = last(j)

        @pl.when(exists(slot))
        def _():
            dk, dv = gradients(slot, pair * 2, 2)
            dkv[slot, 0] = (dkv[slot, 0].astype(F32) + dk).astype(BF)
            dkv[slot, 1] = (dkv[slot, 1].astype(F32) + dv).astype(BF)

            @pl.when(j == 0)
            def _():
                add(slot, 0)
                give(slot, 3, 3, base + b).start()

            @pl.when(j == 1)
            def _():
                add(slot, 1)
                give(slot, 5, 5, base + a).start()

            @pl.when(j == 2)
            def _():
                give(slot, 4, 4, base + b).start()

            @pl.when(j == 3)
            def _():
                for box, d in ((2, a), (3, b)):

                    @pl.when(d < place)
                    def _():
                        add(0, box)

                give(0, 7, 6, position - w).start()

            @pl.when(j == 4)
            def _():
                for box, d in ((2, a), (3, b)):

                    @pl.when(d > place)
                    def _():
                        add(2 * w, box)

                give(2 * w, 6, 7, position + w).start()

    turn_back(mate)
    dq_copy(mate, me, mate).start()
    turn_back(me)
    dq_own = pltpu.make_async_copy(dq.at[me], dquery.at[:, aligned(me, dm.group), :], local.at[8])
    dq_own.start()

    total[...] = dkv[w].astype(F32)
    for box in (5, 4):
        taken(box)
        total[...] += inbox[box].astype(F32)

    @pl.when(has_before)
    def _():
        taken(6)
        total[...] += inbox[6].astype(F32)

    @pl.when(has_after)
    def _():
        taken(7)
        total[...] += inbox[7].astype(F32)

    for part in range(2):
        rows = total[part].T.astype(BF)
        for g in range(n):
            heads[g, part] = rows[g * dm.tokens:(g + 1) * dm.tokens, :]

    def head_copy(g, source, to):
        return remote(heads.at[g], landed.at[source], s_h.at[g], r_h.at[source], head=to)

    for g in peers:
        head_copy(g, me, g).start()
    head_own = pltpu.make_async_copy(heads.at[me], landed.at[me], local.at[9])
    head_own.start()
    head_own.wait()
    for g in peers:
        head_copy(me, g, g).wait_recv()
    for part, out in ((0, dkeys), (1, dvalues)):
        for g in range(n):
            wide[pl.ds(g, dm.tokens, stride=dm.kv_heads), :] = landed[g, part].astype(F32)
        out[...] = wide[...].astype(BF)

    dq_own.wait()
    for g in peers:
        for make in (k_copy, v_copy, q_copy, do_copy, de_copy, dq_copy, head_copy):
            make(g, me, g).wait_send()
        dq_copy(me, g, g).wait_recv()
    for part in range(2):
        for group in (from_own, from_first, from_second):
            group(part, lambda copy: copy.wait_send())

    @pl.when(has_before)
    def _():
        give(0, 7, 6, position - w).wait_send()

    @pl.when(has_after)
    def _():
        give(2 * w, 6, 7, position + w).wait_send()

    for j in range(w + 1):
        slot = [side(o), same(o), side(a), side(b), same(b)][j]

        @pl.when(exists(slot))
        def _():
            give(slot, j, j, base + [a, b, a, b, b][j]).wait_send()

    give(same(a), 5, 5, base + a).wait_send()


def fused(dm, query, keys, values, output, dout):
    n, w, dma = dm.n_head, dm.reach, pltpu.SemaphoreType.DMA
    flat = dm.tokens * dm.kv_heads
    span = dm.slots * dm.block
    chunked = (n, dm.tokens, dm.group, dm.width)
    terms = (2, dm.width, dm.block)
    return pl.pallas_call(
        functools.partial(kernel, dm),
        out_shape=(
            jax.ShapeDtypeStruct(query.shape, BF),
            jax.ShapeDtypeStruct((flat, dm.width), BF),
            jax.ShapeDtypeStruct((flat, dm.width), BF),
        ),
        in_specs=[ANY] * 5,
        out_specs=[ANY, VMEM, VMEM],
        scratch_shapes=[
            pltpu.VMEM((flat, dm.width), BF),
            pltpu.VMEM((flat, dm.width), BF),
            pltpu.VMEM((n, 2, dm.tokens, dm.width), BF),
            pltpu.VMEM((flat, dm.width), F32),
            pltpu.VMEM((n, 1, dm.chunk), F32),
            pltpu.VMEM(query.shape, BF),
            pltpu.VMEM(query.shape, BF),
            pltpu.VMEM(chunked, BF),
            pltpu.VMEM(chunked, BF),
            pltpu.VMEM((n, 1, dm.chunk), F32),
            pltpu.VMEM((dm.slots, 2, dm.block, dm.width), BF),
            pltpu.VMEM((dm.width, span), BF),
            pltpu.VMEM((dm.width, dm.rows), BF),
            pltpu.VMEM((dm.width, dm.rows), BF),
            pltpu.VMEM((span, dm.rows), BF),
            pltpu.VMEM((2, dm.block, dm.score_tile), F32),
            pltpu.VMEM((2, dm.block, dm.grad_tile), BF),
            pltpu.VMEM((dm.slots, dm.rows), F32),
            pltpu.VMEM((dm.slots, dm.rows), F32),
            pltpu.VMEM((dm.slots, dm.rows), F32),
            pltpu.VMEM((dm.width, dm.rows), F32),
            pltpu.VMEM((dm.slots,) + terms, BF),
            pltpu.VMEM((2 * w,) + terms, BF),
            pltpu.VMEM(terms, F32),
            pltpu.VMEM((n, 2, dm.tokens, dm.width), BF),
            pltpu.VMEM((n, 2, dm.tokens, dm.width), BF),
            pltpu.VMEM(chunked, BF),
            dma((11,)),
        ]
        + [dma((2, n))] * 2
        + [dma((n,))] * 10
        + [dma((2, 8)), dma((2, dm.slots)), dma((8,)), dma((8,))],
        compiler_params=pltpu.CompilerParams(
            collective_id=0, has_side_effects=True, vmem_limit_bytes=63 * 2**20
        ),
        name="banded_attention_gradients",
    )(
        query,
        dout,
        output,
        keys.reshape(flat, dm.width),
        values.reshape(flat, dm.width),
    )


def solution(mesh):
    def on_device(query, keys, values, output, dout):
        dm = Dims(query, keys, mesh)
        dquery, dkeys, dvalues = fused(dm, query, keys, values, output, dout)
        return dquery, dkeys.reshape(keys.shape), dvalues.reshape(values.shape)

    spec = P(("blk", "head"), None, None)
    return jax.shard_map(
        on_device, mesh=mesh, in_specs=(spec,) * 5, out_specs=(spec,) * 3, check_vma=False
    )
```

```python
import functools
import math

import jax
import jax.numpy as jnp
from jax import lax
from jax.experimental import pallas as pl
from jax.experimental.pallas import tpu as pltpu
from jax.sharding import PartitionSpec as P

BF = jnp.bfloat16
F32 = jnp.float32
MINOR = (((1,), (1,)), ((), ()))
MESH = pl.DeviceIdType.MESH
ANY = pl.BlockSpec(memory_space=pl.ANY)
VMEM = pl.BlockSpec(memory_space=pltpu.VMEM)


class Dims:
    def __init__(self, query, keys, mesh):
        self.tokens, self.q_heads, self.width = query.shape
        self.kv_heads = keys.shape[1]
        self.n_head = mesh.shape["head"]
        self.n_blk = mesh.shape["blk"]
        self.reach = self.n_blk // 8
        self.slots = 2 * self.reach + 1
        self.block = self.tokens * self.n_head
        self.group = self.q_heads // self.n_head
        self.chunk = self.tokens * self.group
        self.rows = self.chunk * self.n_head
        self.scaling = self.width ** (-0.5)
        self.log2_scaling = self.scaling * math.log2(math.e)
        self.score_tile = 256
        self.grad_tile = 256


def aligned(index, size):
    return pl.ds(pl.multiple_of(index * size, size), size)


def remote(src, dst, send, recv, head=None, blk=None):
    where = {}
    if head is not None:
        where["head"] = head
    if blk is not None:
        where["blk"] = blk
    return pltpu.make_async_remote_copy(
        src_ref=src, dst_ref=dst, send_sem=send, recv_sem=recv, device_id=where, device_id_type=MESH
    )


def split_heads(dm, source, staged, wide, part):
    wide[...] = source[...].astype(F32)
    for g in range(dm.n_head):
        staged[g, part] = wide[pl.ds(g, dm.tokens, stride=dm.kv_heads), :].astype(BF)


def delta_rows(dm, dout, output, rows):
    ones = jnp.ones((8, dm.width), BF)
    for g in range(dm.n_head):
        heads = slice(g * dm.group, (g + 1) * dm.group)
        product = dout[:, heads, :].astype(F32) * output[:, heads, :].astype(F32)
        product = product.reshape(dm.chunk, dm.width)
        high = product.astype(BF)
        low = (product - high.astype(F32)).astype(BF)
        total = lax.dot_general(ones, high, MINOR, preferred_element_type=F32) + lax.dot_general(
            ones, low, MINOR, preferred_element_type=F32
        )
        rows[g] = total[0:1, :].astype(BF).astype(F32)


def score_phase(dm, keys, q_t, probs, scores, tops, sums, b, chunk, count):
    block, tile = dm.block, dm.score_tile
    count = count * dm.chunk // tile
    start = chunk * (dm.chunk // tile)
    step = 32
    top = None
    for i in range(count + 1):
        before = top
        if i < count:
            columns = aligned(start + i, tile)
            x = jnp.dot(keys, q_t[:, columns], preferred_element_type=F32)
            scores[i % 2] = x
            top = jnp.max(jnp.max(x.reshape(block // 8, 8, tile), axis=0), axis=0, keepdims=True)
        if i > 0:
            columns = aligned(start + i - 1, tile)
            total = jnp.zeros((8, tile), F32)
            for at in range(0, block, step):
                p = jnp.exp2((scores[(i - 1) % 2, at:at + step] - before) * dm.log2_scaling)
                total = total + jnp.sum(p.reshape(step // 8, 8, tile), axis=0)
                probs[aligned(b * (block // step) + at // step, step), columns] = p.astype(BF)
            tops[pl.ds(b, 1), columns] = before
            sums[pl.ds(b, 1), columns] = jnp.sum(total, axis=0, keepdims=True)


def combine(dm, tops, sums, factors):
    top = tops[...]
    weight = jnp.exp2((top - jnp.max(top, axis=0, keepdims=True)) * dm.log2_scaling)
    factors[...] = weight / jnp.sum(weight * sums[...], axis=0, keepdims=True)


def gradient_phase(dm, keys_t, values, q_t, do_t, delta, probs, factors, dq_t, small, b, chunk, count):
    block, tile = dm.block, dm.grad_tile
    per_chunk = dm.chunk // tile
    count = count * per_chunk
    start = chunk * per_chunk
    rows = aligned(b, block)
    dk = jnp.zeros((dm.width, block), F32)
    dv = jnp.zeros((dm.width, block), F32)
    for i in range(count + 1):
        if i < count:
            columns = aligned(start + i, tile)
            inner = slice((i % per_chunk) * tile, (i % per_chunk + 1) * tile)
            prob_grad = jnp.dot(values, do_t[:, columns], preferred_element_type=F32)
            grad = probs[rows, columns].astype(F32) * (prob_grad - delta[chunk + i // per_chunk, :, inner])
            small[i % 2] = grad.astype(BF)
        if i > 0:
            columns = aligned(start + i - 1, tile)
            factor = factors[pl.ds(b, 1), columns]
            scaled = factor * dm.scaling
            grad = small[(i - 1) % 2]
            do_scaled = (do_t[:, columns].astype(F32) * factor).astype(BF)
            q_scaled = (q_t[:, columns].astype(F32) * scaled).astype(BF)
            dv = dv + lax.dot_general(do_scaled, probs[rows, columns], MINOR, preferred_element_type=F32)
            dk = dk + lax.dot_general(q_scaled, grad, MINOR, preferred_element_type=F32)
            dq_t[:, columns] += jnp.dot(keys_t, grad, preferred_element_type=F32) * scaled
    return dk, dv


def pick(index, choices):
    value = choices[-1]
    for at in range(len(choices) - 2, -1, -1):
        value = jnp.where(index == at, choices[at], value)
    return value


def kernel(dm, query, dout, output, keys, values, dquery, dkeys, dvalues,
           keys_v, values_v, staged, wide, drow, dout_v, output_v, q_in, do_in, delta, kv,
           keys_t, q_t, do_t, probs, scores, small, tops, sums, factors, dq_t,
           dkv, inbox, total, heads, landed, dq,
           local, s_kv, r_kv, s_q, r_q, s_do, r_do, s_de, r_de, s_dq, r_dq, s_h, r_h,
           s_hop, r_n, s_out, r_box):
    me = lax.axis_index("head")
    position = lax.axis_index("blk")
    n, w = dm.n_head, dm.reach
    pair = me // 2
    core = lax.rem(me, 2)
    mate = pair * 2 + 1 - core
    across = [(1 - pair) * 2 + core, (1 - pair) * 2 + 1 - core]
    peers = [mate] + across
    place = lax.rem(position, w)
    a = place + 1 - 2 * lax.rem(place, 2)
    b = w - 1 - place
    o = lax.rem(place + 2, w)
    has_before = position - w >= 0
    has_after = position + w < dm.n_blk
    base = position - place

    def same(d):
        return w + d - place

    def side(d):
        return lax.rem(d - place + 2 * w, 2 * w)

    def exists(slot):
        other = position - w + slot
        return (other >= 0) & (other < dm.n_blk)

    own = [
        pltpu.make_async_copy(keys, keys_v, local.at[0]),
        pltpu.make_async_copy(values, values_v, local.at[1]),
        pltpu.make_async_copy(dout, dout_v, local.at[2]),
        pltpu.make_async_copy(output, output_v, local.at[3]),
        pltpu.make_async_copy(query.at[:, aligned(me, dm.group), :], q_in.at[me], local.at[4]),
        pltpu.make_async_copy(dout.at[:, aligned(me, dm.group), :], do_in.at[me], local.at[5]),
    ]
    for copy in own:
        copy.start()
    barrier = pltpu.get_barrier_semaphore()
    for g in peers:
        pl.semaphore_signal(barrier, inc=1, device_id={"head": g}, device_id_type=MESH)
    for c in (a, b):
        pl.semaphore_signal(barrier, inc=1, device_id={"blk": base + c}, device_id_type=MESH)

    @pl.when(has_before)
    def _():
        pl.semaphore_signal(barrier, inc=1, device_id={"blk": position - w}, device_id_type=MESH)

    @pl.when(has_after)
    def _():
        pl.semaphore_signal(barrier, inc=1, device_id={"blk": position + w}, device_id_type=MESH)

    own[0].wait()
    split_heads(dm, keys_v, staged, wide, 0)
    groups = position // w
    ends = jnp.minimum(groups, 1) + jnp.minimum(dm.n_blk // w - 1 - groups, 1)
    pl.semaphore_wait(barrier, n - 1 + 2 + ends)

    def part_copy(part, g, source, to):
        return remote(staged.at[g, part], kv.at[w, part, aligned(source, dm.tokens), :],
                      s_kv.at[part, g], r_kv.at[part, source], head=to)

    def k_copy(g, source, to):
        return part_copy(0, g, source, to)

    def v_copy(g, source, to):
        return part_copy(1, g, source, to)

    def q_copy(g, source, to):
        return remote(query.at[:, aligned(g, dm.group), :], q_in.at[source], s_q.at[g], r_q.at[source], head=to)

    def do_copy(g, source, to):
        return remote(dout.at[:, aligned(g, dm.group), :], do_in.at[source], s_do.at[g], r_do.at[source], head=to)

    def de_copy(g, source, to):
        return remote(drow.at[g], delta.at[source], s_de.at[g], r_de.at[source], head=to)

    for g in peers:
        k_copy(g, me, g).start()
    k_own = pltpu.make_async_copy(staged.at[me, 0], kv.at[w, 0, aligned(me, dm.tokens), :], local.at[6])
    k_own.start()
    q_copy(mate, me, mate).start()
    own[1].wait()
    split_heads(dm, values_v, staged, wide, 1)
    for g in peers:
        v_copy(g, me, g).start()
    v_own = pltpu.make_async_copy(staged.at[me, 1], kv.at[w, 1, aligned(me, dm.tokens), :], local.at[10])
    v_own.start()
    own[4].wait()

    def turn(source, target, g):
        target[:, aligned(g, dm.chunk)] = source[g].astype(F32).reshape(dm.chunk, dm.width).T.astype(BF)

    turn(q_in, q_t, me)
    k_own.wait()
    for g in peers:
        k_copy(me, g, g).wait_recv()

    def hop(part, source, slot, k, to):
        return remote(kv.at[source, part], kv.at[slot, part], s_hop.at[part, k], r_n.at[part, slot], blk=to)

    def arrived(part, slot):
        hop(part, slot, slot, 0, base + a).wait_recv()

    def from_own(part, act):
        act(hop(part, w, w + place - a, 0, base + a))
        act(hop(part, w, w + place - b, 1, base + b))

        @pl.when(has_before)
        def _():
            act(hop(part, w, 2 * w, 2, position - w))

        @pl.when(has_after)
        def _():
            act(hop(part, w, 0, 3, position + w))

    def from_first(part, act):
        for k, d in enumerate((a, b)):

            @pl.when(has_before & (d < place))
            def _():
                act(hop(part, 0, place - d, 4 + k, base + d))

            @pl.when(has_after & (d > place))
            def _():
                act(hop(part, 2 * w, 2 * w + place - d, 4 + k, base + d))

        act(hop(part, same(a), w + a - b, 6, base + b))

    def from_second(part, act):
        @pl.when(exists(side(b)))
        def _():
            act(hop(part, side(b), lax.rem(b - a + 2 * w, 2 * w), 7, base + a))

    def pass_first(part):
        @pl.when(has_before)
        def _():
            arrived(part, 0)

        @pl.when(has_after)
        def _():
            arrived(part, 2 * w)

        arrived(part, same(a))
        from_first(part, lambda copy: copy.start())

    def pass_second(part):
        @pl.when(exists(side(b)))
        def _():
            arrived(part, side(b))

        from_second(part, lambda copy: copy.start())

    from_own(0, lambda copy: copy.start())
    for g in across:
        q_copy(g, me, g).start()
    own[2].wait()
    own[3].wait()
    delta_rows(dm, dout_v, output_v, drow)
    for g in peers:
        de_copy(g, me, g).start()
    de_own = pltpu.make_async_copy(drow.at[me], delta.at[me], local.at[7])
    de_own.start()
    for at in range(0, dm.rows, 512):
        dq_t[:, at:at + 512] = jnp.zeros((dm.width, 512), F32)
    tops[...] = jnp.full((dm.slots, dm.rows), -jnp.inf, F32)
    sums[...] = jnp.zeros((dm.slots, dm.rows), F32)
    q_copy(me, mate, mate).wait_recv()
    turn(q_in, q_t, mate)

    def order(j):
        return pick(j, [jnp.int32(w), same(a), same(b), jnp.int32(0), jnp.int32(2 * w),
                        side(b), side(a), same(o), side(o)])

    @pl.loop(0, dm.slots)
    def _(j):
        slot = order(j)

        @pl.when(j == 1)
        def _():
            pass_first(0)
            arrived(0, same(b))
            v_own.wait()
            for g in peers:
                v_copy(me, g, g).wait_recv()
            from_own(1, lambda copy: copy.start())

        @pl.when(j == 5)
        def _():
            pass_second(0)

        @pl.when(exists(slot))
        def _():
            @pl.when(j > 5)
            def _():
                arrived(0, slot)

            keys_t[:, aligned(slot, dm.block)] = kv[slot, 0].T
            score_phase(dm, kv[slot, 0], q_t, probs, scores, tops, sums, slot, pair * 2, 2)

    for g in across:
        q_copy(me, g, g).wait_recv()
    for g in across + [mate]:
        do_copy(g, me, g).start()
    pass_first(1)
    for g in across:
        turn(q_in, q_t, g)

    @pl.loop(0, dm.slots)
    def _(j):
        slot = order(j)

        @pl.when(j == 6)
        def _():
            pass_second(1)

        @pl.when(exists(slot))
        def _():
            score_phase(dm, kv[slot, 0], q_t, probs, scores, tops, sums, slot, (1 - pair) * 2, 2)

    combine(dm, tops, sums, factors)
    own[5].wait()
    turn(do_in, do_t, me)
    de_own.wait()
    for g in [mate] + across:
        do_copy(me, g, g).wait_recv()
        de_copy(me, g, g).wait_recv()
        turn(do_in, do_t, g)
    arrived(1, same(b))
    arrived(1, same(o))
    for d in (a, o):

        @pl.when(exists(side(d)))
        def _():
            arrived(1, side(d))

    def give(slot, box, k, to):
        return remote(dkv.at[slot], inbox.at[box], s_out.at[k], r_box.at[box], blk=to)

    def taken(box):
        give(w, box, box, base + a).wait_recv()

    def gradients(slot, chunk, count):
        return gradient_phase(
            dm, keys_t[:, aligned(slot, dm.block)], kv[slot, 1], q_t, do_t, delta, probs, factors, dq_t, small,
            slot, chunk, count
        )

    def first(j):
        return pick(j, [side(o), same(o), side(a)])

    def last(j):
        return pick(j, [side(b), same(a), same(b), jnp.int32(0), jnp.int32(2 * w), jnp.int32(w)])

    def add(slot, box):
        taken(box)
        dkv[slot] = (dkv[slot].astype(F32) + inbox[box].astype(F32)).astype(BF)

    @pl.loop(0, 3)
    def _(j):
        slot = first(j)

        @pl.when(exists(slot))
        def _():
            dk, dv = gradients(slot, 0, 4)
            dkv[slot, 0] = dk.astype(BF)
            dkv[slot, 1] = dv.astype(BF)
            give(slot, j, j, base + pick(j, [a, b, a])).start()

    @pl.loop(0, 6)
    def _(j):
        slot = last(j)

        @pl.when(exists(slot))
        def _():
            dk, dv = gradients(slot, (1 - pair) * 2, 2)
            dkv[slot, 0] = dk.astype(BF)
            dkv[slot, 1] = dv.astype(BF)

    def dq_copy(g, source, to):
        return remote(dq.at[g], dquery.at[:, aligned(source, dm.group), :], s_dq.at[g], r_dq.at[source], head=to)

    def turn_back(g):
        dq[g] = dq_t[:, aligned(g, dm.chunk)].T.reshape(dm.tokens, dm.group, dm.width).astype(BF)

    for g in across:
        turn_back(g)
        dq_copy(g, me, g).start()

    @pl.loop(0, 6)
    def _(j):
        slot = last(j)

        @pl.when(exists(slot))
        def _():
            dk, dv = gradients(slot, pair * 2, 2)
            dkv[slot, 0] = (dkv[slot, 0].astype(F32) + dk).astype(BF)
            dkv[slot, 1] = (dkv[slot, 1].astype(F32) + dv).astype(BF)

            @pl.when(j == 0)
            def _():
                add(slot, 0)
                give(slot, 3, 3, base + b).start()

            @pl.when(j == 1)
            def _():
                add(slot, 1)
                give(slot, 5, 5, base + a).start()

            @pl.when(j == 2)
            def _():
                give(slot, 4, 4, base + b).start()

            @pl.when(j == 3)
            def _():
                for box, d in ((2, a), (3, b)):

                    @pl.when(d < place)
                    def _():
                        add(0, box)

                give(0, 7, 6, position - w).start()

            @pl.when(j == 4)
            def _():
                for box, d in ((2, a), (3, b)):

                    @pl.when(d > place)
                    def _():
                        add(2 * w, box)

                give(2 * w, 6, 7, position + w).start()

    turn_back(mate)
    dq_copy(mate, me, mate).start()
    turn_back(me)
    dq_own = pltpu.make_async_copy(dq.at[me], dquery.at[:, aligned(me, dm.group), :], local.at[8])
    dq_own.start()

    total[...] = dkv[w].astype(F32)
    for box in (5, 4):
        taken(box)
        total[...] += inbox[box].astype(F32)

    @pl.when(has_before)
    def _():
        taken(6)
        total[...] += inbox[6].astype(F32)

    @pl.when(has_after)
    def _():
        taken(7)
        total[...] += inbox[7].astype(F32)

    for part in range(2):
        rows = total[part].T.astype(BF)
        for g in range(n):
            heads[g, part] = rows[g * dm.tokens:(g + 1) * dm.tokens, :]

    def head_copy(g, source, to):
        return remote(heads.at[g], landed.at[source], s_h.at[g], r_h.at[source], head=to)

    for g in peers:
        head_copy(g, me, g).start()
    head_own = pltpu.make_async_copy(heads.at[me], landed.at[me], local.at[9])
    head_own.start()
    head_own.wait()
    for g in peers:
        head_copy(me, g, g).wait_recv()
    for part, out in ((0, dkeys), (1, dvalues)):
        for g in range(n):
            wide[pl.ds(g, dm.tokens, stride=dm.kv_heads), :] = landed[g, part].astype(F32)
        out[...] = wide[...].astype(BF)

    dq_own.wait()
    for g in peers:
        for make in (k_copy, v_copy, q_copy, do_copy, de_copy, dq_copy, head_copy):
            make(g, me, g).wait_send()
        dq_copy(me, g, g).wait_recv()
    for part in range(2):
        for group in (from_own, from_first, from_second):
            group(part, lambda copy: copy.wait_send())

    @pl.when(has_before)
    def _():
        give(0, 7, 6, position - w).wait_send()

    @pl.when(has_after)
    def _():
        give(2 * w, 6, 7, position + w).wait_send()

    for j in range(w + 1):
        slot = [side(o), same(o), side(a), side(b), same(b)][j]

        @pl.when(exists(slot))
        def _():
            give(slot, j, j, base + [a, b, a, b, b][j]).wait_send()

    give(same(a), 5, 5, base + a).wait_send()


def fused(dm, query, keys, values, output, dout):
    n, w, dma = dm.n_head, dm.reach, pltpu.SemaphoreType.DMA
    flat = dm.tokens * dm.kv_heads
    span = dm.slots * dm.block
    chunked = (n, dm.tokens, dm.group, dm.width)
    terms = (2, dm.width, dm.block)
    return pl.pallas_call(
        functools.partial(kernel, dm),
        out_shape=(
            jax.ShapeDtypeStruct(query.shape, BF),
            jax.ShapeDtypeStruct((flat, dm.width), BF),
            jax.ShapeDtypeStruct((flat, dm.width), BF),
        ),
        in_specs=[ANY] * 5,
        out_specs=[ANY, VMEM, VMEM],
        scratch_shapes=[
            pltpu.VMEM((flat, dm.width), BF),
            pltpu.VMEM((flat, dm.width), BF),
            pltpu.VMEM((n, 2, dm.tokens, dm.width), BF),
            pltpu.VMEM((flat, dm.width), F32),
            pltpu.VMEM((n, 1, dm.chunk), F32),
            pltpu.VMEM(query.shape, BF),
            pltpu.VMEM(query.shape, BF),
            pltpu.VMEM(chunked, BF),
            pltpu.VMEM(chunked, BF),
            pltpu.VMEM((n, 1, dm.chunk), F32),
            pltpu.VMEM((dm.slots, 2, dm.block, dm.width), BF),
            pltpu.VMEM((dm.width, span), BF),
            pltpu.VMEM((dm.width, dm.rows), BF),
            pltpu.VMEM((dm.width, dm.rows), BF),
            pltpu.VMEM((span, dm.rows), BF),
            pltpu.VMEM((2, dm.block, dm.score_tile), F32),
            pltpu.VMEM((2, dm.block, dm.grad_tile), BF),
            pltpu.VMEM((dm.slots, dm.rows), F32),
            pltpu.VMEM((dm.slots, dm.rows), F32),
            pltpu.VMEM((dm.slots, dm.rows), F32),
            pltpu.VMEM((dm.width, dm.rows), F32),
            pltpu.VMEM((dm.slots,) + terms, BF),
            pltpu.VMEM((2 * w,) + terms, BF),
            pltpu.VMEM(terms, F32),
            pltpu.VMEM((n, 2, dm.tokens, dm.width), BF),
            pltpu.VMEM((n, 2, dm.tokens, dm.width), BF),
            pltpu.VMEM(chunked, BF),
            dma((11,)),
        ]
        + [dma((2, n))] * 2
        + [dma((n,))] * 10
        + [dma((2, 8)), dma((2, dm.slots)), dma((8,)), dma((8,))],
        compiler_params=pltpu.CompilerParams(
            collective_id=0, has_side_effects=True, vmem_limit_bytes=63 * 2**20
        ),
        name="banded_attention_gradients",
    )(
        query,
        dout,
        output,
        keys.reshape(flat, dm.width),
        values.reshape(flat, dm.width),
    )


def solution(mesh):
    def on_device(query, keys, values, output, dout):
        dm = Dims(query, keys, mesh)
        dquery, dkeys, dvalues = fused(dm, query, keys, values, output, dout)
        return dquery, dkeys.reshape(keys.shape), dvalues.reshape(values.shape)

    spec = P(("blk", "head"), None, None)
    return jax.shard_map(
        on_device, mesh=mesh, in_specs=(spec,) * 5, out_specs=(spec,) * 3, check_vma=False
    )
```

```python
import functools
import math

import jax
import jax.numpy as jnp
from jax import lax
from jax.experimental import pallas as pl
from jax.experimental.pallas import tpu as pltpu
from jax.sharding import PartitionSpec as P

BF = jnp.bfloat16
F32 = jnp.float32
MINOR = (((1,), (1,)), ((), ()))
MESH = pl.DeviceIdType.MESH
ANY = pl.BlockSpec(memory_space=pl.ANY)
VMEM = pl.BlockSpec(memory_space=pltpu.VMEM)


class Dims:
    def __init__(self, query, keys, mesh):
        self.tokens, self.q_heads, self.width = query.shape
        self.kv_heads = keys.shape[1]
        self.n_head = mesh.shape["head"]
        self.n_blk = mesh.shape["blk"]
        self.reach = self.n_blk // 8
        self.slots = 2 * self.reach + 1
        self.block = self.tokens * self.n_head
        self.group = self.q_heads // self.n_head
        self.chunk = self.tokens * self.group
        self.rows = self.chunk * self.n_head
        self.scaling = self.width ** (-0.5)
        self.log2_scaling = self.scaling * math.log2(math.e)
        self.score_tile = 256
        self.grad_tile = 256


def aligned(index, size):
    return pl.ds(pl.multiple_of(index * size, size), size)


def remote(src, dst, send, recv, head=None, blk=None):
    where = {}
    if head is not None:
        where["head"] = head
    if blk is not None:
        where["blk"] = blk
    return pltpu.make_async_remote_copy(
        src_ref=src, dst_ref=dst, send_sem=send, recv_sem=recv, device_id=where, device_id_type=MESH
    )


def split_heads(dm, source, staged, wide, part):
    wide[...] = source[...].astype(F32)
    for g in range(dm.n_head):
        staged[g, part] = wide[pl.ds(g, dm.tokens, stride=dm.kv_heads), :].astype(BF)


def delta_rows(dm, dout, output, rows):
    ones = jnp.ones((8, dm.width), BF)
    for g in range(dm.n_head):
        heads = slice(g * dm.group, (g + 1) * dm.group)
        product = dout[:, heads, :].astype(F32) * output[:, heads, :].astype(F32)
        product = product.reshape(dm.chunk, dm.width)
        high = product.astype(BF)
        low = (product - high.astype(F32)).astype(BF)
        total = lax.dot_general(ones, high, MINOR, preferred_element_type=F32) + lax.dot_general(
            ones, low, MINOR, preferred_element_type=F32
        )
        rows[g] = total[0:1, :].astype(BF).astype(F32)


def score_phase(dm, keys, q_t, probs, scores, tops, sums, b, chunk, count):
    block, tile = dm.block, dm.score_tile
    count = count * dm.chunk // tile
    start = chunk * (dm.chunk // tile)
    step = 32
    top = None
    for i in range(count + 1):
        before = top
        if i < count:
            columns = aligned(start + i, tile)
            x = jnp.dot(keys, q_t[:, columns], preferred_element_type=F32)
            scores[i % 2] = x
            top = jnp.max(jnp.max(x.reshape(block // 8, 8, tile), axis=0), axis=0, keepdims=True)
        if i > 0:
            columns = aligned(start + i - 1, tile)
            total = jnp.zeros((8, tile), F32)
            for at in range(0, block, step):
                p = jnp.exp2((scores[(i - 1) % 2, at:at + step] - before) * dm.log2_scaling)
                total = total + jnp.sum(p.reshape(step // 8, 8, tile), axis=0)
                probs[aligned(b * (block // step) + at // step, step), columns] = p.astype(BF)
            tops[pl.ds(b, 1), columns] = before
            sums[pl.ds(b, 1), columns] = jnp.sum(total, axis=0, keepdims=True)


def combine(dm, tops, sums, factors):
    top = tops[...]
    weight = jnp.exp2((top - jnp.max(top, axis=0, keepdims=True)) * dm.log2_scaling)
    factors[...] = weight / jnp.sum(weight * sums[...], axis=0, keepdims=True)


def gradient_phase(dm, keys_t, values, q_t, do_t, delta, probs, factors, dq_t, small, b, chunk, count):
    block, tile = dm.block, dm.grad_tile
    per_chunk = dm.chunk // tile
    count = count * per_chunk
    start = chunk * per_chunk
    rows = aligned(b, block)
    dk = jnp.zeros((dm.width, block), F32)
    dv = jnp.zeros((dm.width, block), F32)
    for i in range(count + 1):
        if i < count:
            columns = aligned(start + i, tile)
            inner = slice((i % per_chunk) * tile, (i % per_chunk + 1) * tile)
            prob_grad = jnp.dot(values, do_t[:, columns], preferred_element_type=F32)
            grad = probs[rows, columns].astype(F32) * (prob_grad - delta[chunk + i // per_chunk, :, inner])
            small[i % 2] = grad.astype(BF)
        if i > 0:
            columns = aligned(start + i - 1, tile)
            factor = factors[pl.ds(b, 1), columns]
            scaled = factor * dm.scaling
            grad = small[(i - 1) % 2]
            do_scaled = (do_t[:, columns].astype(F32) * factor).astype(BF)
            q_scaled = (q_t[:, columns].astype(F32) * scaled).astype(BF)
            dv = dv + lax.dot_general(do_scaled, probs[rows, columns], MINOR, preferred_element_type=F32)
            dk = dk + lax.dot_general(q_scaled, grad, MINOR, preferred_element_type=F32)
            dq_t[:, columns] += jnp.dot(keys_t, grad, preferred_element_type=F32) * scaled
    return dk, dv


def pick(index, choices):
    value = choices[-1]
    for at in range(len(choices) - 2, -1, -1):
        value = jnp.where(index == at, choices[at], value)
    return value


def kernel(dm, query, dout, output, keys, values, dquery, dkeys, dvalues,
           keys_v, values_v, staged, wide, drow, dout_v, output_v, q_in, do_in, delta, kv,
           keys_t, q_t, do_t, probs, scores, small, tops, sums, factors, dq_t,
           dkv, inbox, total, heads, landed, dq,
           local, s_kv, r_kv, s_q, r_q, s_do, r_do, s_de, r_de, s_dq, r_dq, s_h, r_h,
           s_hop, r_n, s_out, r_box):
    me = lax.axis_index("head")
    position = lax.axis_index("blk")
    n, w = dm.n_head, dm.reach
    pair = me // 2
    core = lax.rem(me, 2)
    mate = pair * 2 + 1 - core
    across = [(1 - pair) * 2 + core, (1 - pair) * 2 + 1 - core]
    peers = [mate] + across
    place = lax.rem(position, w)
    a = place + 1 - 2 * lax.rem(place, 2)
    b = w - 1 - place
    o = lax.rem(place + 2, w)
    has_before = position - w >= 0
    has_after = position + w < dm.n_blk
    base = position - place

    def same(d):
        return w + d - place

    def side(d):
        return lax.rem(d - place + 2 * w, 2 * w)

    def exists(slot):
        other = position - w + slot
        return (other >= 0) & (other < dm.n_blk)

    own = [
        pltpu.make_async_copy(keys, keys_v, local.at[0]),
        pltpu.make_async_copy(values, values_v, local.at[1]),
        pltpu.make_async_copy(dout, dout_v, local.at[2]),
        pltpu.make_async_copy(output, output_v, local.at[3]),
        pltpu.make_async_copy(query.at[:, aligned(me, dm.group), :], q_in.at[me], local.at[4]),
        pltpu.make_async_copy(dout.at[:, aligned(me, dm.group), :], do_in.at[me], local.at[5]),
    ]
    for copy in own:
        copy.start()
    barrier = pltpu.get_barrier_semaphore()
    for g in peers:
        pl.semaphore_signal(barrier, inc=1, device_id={"head": g}, device_id_type=MESH)
    for c in (a, b):
        pl.semaphore_signal(barrier, inc=1, device_id={"blk": base + c}, device_id_type=MESH)

    @pl.when(has_before)
    def _():
        pl.semaphore_signal(barrier, inc=1, device_id={"blk": position - w}, device_id_type=MESH)

    @pl.when(has_after)
    def _():
        pl.semaphore_signal(barrier, inc=1, device_id={"blk": position + w}, device_id_type=MESH)

    own[0].wait()
    split_heads(dm, keys_v, staged, wide, 0)
    groups = position // w
    ends = jnp.minimum(groups, 1) + jnp.minimum(dm.n_blk // w - 1 - groups, 1)
    pl.semaphore_wait(barrier, n - 1 + 2 + ends)

    def part_copy(part, g, source, to):
        return remote(staged.at[g, part], kv.at[w, part, aligned(source, dm.tokens), :],
                      s_kv.at[part, g], r_kv.at[part, source], head=to)

    def k_copy(g, source, to):
        return part_copy(0, g, source, to)

    def v_copy(g, source, to):
        return part_copy(1, g, source, to)

    def q_copy(g, source, to):
        return remote(query.at[:, aligned(g, dm.group), :], q_in.at[source], s_q.at[g], r_q.at[source], head=to)

    def do_copy(g, source, to):
        return remote(dout.at[:, aligned(g, dm.group), :], do_in.at[source], s_do.at[g], r_do.at[source], head=to)

    def de_copy(g, source, to):
        return remote(drow.at[g], delta.at[source], s_de.at[g], r_de.at[source], head=to)

    for g in peers:
        k_copy(g, me, g).start()
    k_own = pltpu.make_async_copy(staged.at[me, 0], kv.at[w, 0, aligned(me, dm.tokens), :], local.at[6])
    k_own.start()
    q_copy(mate, me, mate).start()
    own[1].wait()
    split_heads(dm, values_v, staged, wide, 1)
    for g in peers:
        v_copy(g, me, g).start()
    v_own = pltpu.make_async_copy(staged.at[me, 1], kv.at[w, 1, aligned(me, dm.tokens), :], local.at[10])
    v_own.start()
    own[4].wait()

    def turn(source, target, g):
        target[:, aligned(g, dm.chunk)] = source[g].astype(F32).reshape(dm.chunk, dm.width).T.astype(BF)

    turn(q_in, q_t, me)
    k_own.wait()
    for g in peers:
        k_copy(me, g, g).wait_recv()

    def hop(part, source, slot, k, to):
        return remote(kv.at[source, part], kv.at[slot, part], s_hop.at[part, k], r_n.at[part, slot], blk=to)

    def arrived(part, slot):
        hop(part, slot, slot, 0, base + a).wait_recv()

    def from_own(part, act):
        act(hop(part, w, w + place - a, 0, base + a))
        act(hop(part, w, w + place - b, 1, base + b))

        @pl.when(has_before)
        def _():
            act(hop(part, w, 2 * w, 2, position - w))

        @pl.when(has_after)
        def _():
            act(hop(part, w, 0, 3, position + w))

    def from_first(part, act):
        for k, d in enumerate((a, b)):

            @pl.when(has_before & (d < place))
            def _():
                act(hop(part, 0, place - d, 4 + k, base + d))

            @pl.when(has_after & (d > place))
            def _():
                act(hop(part, 2 * w, 2 * w + place - d, 4 + k, base + d))

        act(hop(part, same(a), w + a - b, 6, base + b))

    def from_second(part, act):
        @pl.when(exists(side(b)))
        def _():
            act(hop(part, side(b), lax.rem(b - a + 2 * w, 2 * w), 7, base + a))

    def pass_first(part):
        @pl.when(has_before)
        def _():
            arrived(part, 0)

        @pl.when(has_after)
        def _():
            arrived(part, 2 * w)

        arrived(part, same(a))
        from_first(part, lambda copy: copy.start())

    def pass_second(part):
        @pl.when(exists(side(b)))
        def _():
            arrived(part, side(b))

        from_second(part, lambda copy: copy.start())

    from_own(0, lambda copy: copy.start())
    for g in across:
        q_copy(g, me, g).start()
    own[2].wait()
    own[3].wait()
    delta_rows(dm, dout_v, output_v, drow)
    for g in peers:
        de_copy(g, me, g).start()
    de_own = pltpu.make_async_copy(drow.at[me], delta.at[me], local.at[7])
    de_own.start()
    for at in range(0, dm.rows, 512):
        dq_t[:, at:at + 512] = jnp.zeros((dm.width, 512), F32)
    tops[...] = jnp.full((dm.slots, dm.rows), -jnp.inf, F32)
    sums[...] = jnp.zeros((dm.slots, dm.rows), F32)
    q_copy(me, mate, mate).wait_recv()
    turn(q_in, q_t, mate)

    def order(j):
        return pick(j, [jnp.int32(w), same(a), same(b), jnp.int32(0), jnp.int32(2 * w),
                        side(b), side(a), same(o), side(o)])

    @pl.loop(0, dm.slots)
    def _(j):
        slot = order(j)

        @pl.when(j == 1)
        def _():
            pass_first(0)
            v_own.wait()
            for g in peers:
                v_copy(me, g, g).wait_recv()
            from_own(1, lambda copy: copy.start())

        @pl.when(j == 5)
        def _():
            pass_second(0)

        @pl.when(exists(slot))
        def _():
            @pl.when((j > 5) | (j == 2))
            def _():
                arrived(0, slot)

            keys_t[:, aligned(slot, dm.block)] = kv[slot, 0].T
            score_phase(dm, kv[slot, 0], q_t, probs, scores, tops, sums, slot, pair * 2, 2)

    for g in across:
        q_copy(me, g, g).wait_recv()
    for g in across + [mate]:
        do_copy(g, me, g).start()
    pass_first(1)
    for g in across:
        turn(q_in, q_t, g)

    @pl.loop(0, dm.slots)
    def _(j):
        slot = order(j)

        @pl.when(j == 6)
        def _():
            pass_second(1)

        @pl.when(exists(slot))
        def _():
            score_phase(dm, kv[slot, 0], q_t, probs, scores, tops, sums, slot, (1 - pair) * 2, 2)

    combine(dm, tops, sums, factors)
    own[5].wait()
    turn(do_in, do_t, me)
    de_own.wait()
    for g in [mate] + across:
        do_copy(me, g, g).wait_recv()
        de_copy(me, g, g).wait_recv()
        turn(do_in, do_t, g)
    arrived(1, same(b))
    arrived(1, same(o))
    for d in (a, o):

        @pl.when(exists(side(d)))
        def _():
            arrived(1, side(d))

    def give(slot, box, k, to):
        return remote(dkv.at[slot], inbox.at[box], s_out.at[k], r_box.at[box], blk=to)

    def taken(box):
        give(w, box, box, base + a).wait_recv()

    def gradients(slot, chunk, count):
        return gradient_phase(
            dm, keys_t[:, aligned(slot, dm.block)], kv[slot, 1], q_t, do_t, delta, probs, factors, dq_t, small,
            slot, chunk, count
        )

    def first(j):
        return pick(j, [side(o), same(o), side(a)])

    def last(j):
        return pick(j, [side(b), same(a), same(b), jnp.int32(0), jnp.int32(2 * w), jnp.int32(w)])

    def add(slot, box):
        taken(box)
        dkv[slot] = (dkv[slot].astype(F32) + inbox[box].astype(F32)).astype(BF)

    @pl.loop(0, 3)
    def _(j):
        slot = first(j)

        @pl.when(exists(slot))
        def _():
            dk, dv = gradients(slot, 0, 4)
            dkv[slot, 0] = dk.astype(BF)
            dkv[slot, 1] = dv.astype(BF)
            give(slot, j, j, base + pick(j, [a, b, a])).start()

    @pl.loop(0, 6)
    def _(j):
        slot = last(j)

        @pl.when(exists(slot))
        def _():
            dk, dv = gradients(slot, (1 - pair) * 2, 2)
            dkv[slot, 0] = dk.astype(BF)
            dkv[slot, 1] = dv.astype(BF)

    def dq_copy(g, source, to):
        return remote(dq.at[g], dquery.at[:, aligned(source, dm.group), :], s_dq.at[g], r_dq.at[source], head=to)

    def turn_back(g):
        dq[g] = dq_t[:, aligned(g, dm.chunk)].T.reshape(dm.tokens, dm.group, dm.width).astype(BF)

    for g in across:
        turn_back(g)
        dq_copy(g, me, g).start()

    @pl.loop(0, 6)
    def _(j):
        slot = last(j)

        @pl.when(exists(slot))
        def _():
            dk, dv = gradients(slot, pair * 2, 2)
            dkv[slot, 0] = (dkv[slot, 0].astype(F32) + dk).astype(BF)
            dkv[slot, 1] = (dkv[slot, 1].astype(F32) + dv).astype(BF)

            @pl.when(j == 0)
            def _():
                add(slot, 0)
                give(slot, 3, 3, base + b).start()

            @pl.when(j == 1)
            def _():
                add(slot, 1)
                give(slot, 5, 5, base + a).start()

            @pl.when(j == 2)
            def _():
                give(slot, 4, 4, base + b).start()

            @pl.when(j == 3)
            def _():
                for box, d in ((2, a), (3, b)):

                    @pl.when(d < place)
                    def _():
                        add(0, box)

                give(0, 7, 6, position - w).start()

            @pl.when(j == 4)
            def _():
                for box, d in ((2, a), (3, b)):

                    @pl.when(d > place)
                    def _():
                        add(2 * w, box)

                give(2 * w, 6, 7, position + w).start()

    turn_back(mate)
    dq_copy(mate, me, mate).start()
    turn_back(me)
    dq_own = pltpu.make_async_copy(dq.at[me], dquery.at[:, aligned(me, dm.group), :], local.at[8])
    dq_own.start()

    total[...] = dkv[w].astype(F32)
    for box in (5, 4):
        taken(box)
        total[...] += inbox[box].astype(F32)

    @pl.when(has_before)
    def _():
        taken(6)
        total[...] += inbox[6].astype(F32)

    @pl.when(has_after)
    def _():
        taken(7)
        total[...] += inbox[7].astype(F32)

    for part in range(2):
        rows = total[part].T.astype(BF)
        for g in range(n):
            heads[g, part] = rows[g * dm.tokens:(g + 1) * dm.tokens, :]

    def head_copy(g, source, to):
        return remote(heads.at[g], landed.at[source], s_h.at[g], r_h.at[source], head=to)

    for g in peers:
        head_copy(g, me, g).start()
    head_own = pltpu.make_async_copy(heads.at[me], landed.at[me], local.at[9])
    head_own.start()
    head_own.wait()
    for g in peers:
        head_copy(me, g, g).wait_recv()
    for part, out in ((0, dkeys), (1, dvalues)):
        for g in range(n):
            wide[pl.ds(g, dm.tokens, stride=dm.kv_heads), :] = landed[g, part].astype(F32)
        out[...] = wide[...].astype(BF)

    dq_own.wait()
    for g in peers:
        for make in (k_copy, v_copy, q_copy, do_copy, de_copy, dq_copy, head_copy):
            make(g, me, g).wait_send()
        dq_copy(me, g, g).wait_recv()
    for part in range(2):
        for group in (from_own, from_first, from_second):
            group(part, lambda copy: copy.wait_send())

    @pl.when(has_before)
    def _():
        give(0, 7, 6, position - w).wait_send()

    @pl.when(has_after)
    def _():
        give(2 * w, 6, 7, position + w).wait_send()

    for j in range(w + 1):
        slot = [side(o), same(o), side(a), side(b), same(b)][j]

        @pl.when(exists(slot))
        def _():
            give(slot, j, j, base + [a, b, a, b, b][j]).wait_send()

    give(same(a), 5, 5, base + a).wait_send()


def fused(dm, query, keys, values, output, dout):
    n, w, dma = dm.n_head, dm.reach, pltpu.SemaphoreType.DMA
    flat = dm.tokens * dm.kv_heads
    span = dm.slots * dm.block
    chunked = (n, dm.tokens, dm.group, dm.width)
    terms = (2, dm.width, dm.block)
    return pl.pallas_call(
        functools.partial(kernel, dm),
        out_shape=(
            jax.ShapeDtypeStruct(query.shape, BF),
            jax.ShapeDtypeStruct((flat, dm.width), BF),
            jax.ShapeDtypeStruct((flat, dm.width), BF),
        ),
        in_specs=[ANY] * 5,
        out_specs=[ANY, VMEM, VMEM],
        scratch_shapes=[
            pltpu.VMEM((flat, dm.width), BF),
            pltpu.VMEM((flat, dm.width), BF),
            pltpu.VMEM((n, 2, dm.tokens, dm.width), BF),
            pltpu.VMEM((flat, dm.width), F32),
            pltpu.VMEM((n, 1, dm.chunk), F32),
            pltpu.VMEM(query.shape, BF),
            pltpu.VMEM(query.shape, BF),
            pltpu.VMEM(chunked, BF),
            pltpu.VMEM(chunked, BF),
            pltpu.VMEM((n, 1, dm.chunk), F32),
            pltpu.VMEM((dm.slots, 2, dm.block, dm.width), BF),
            pltpu.VMEM((dm.width, span), BF),
            pltpu.VMEM((dm.width, dm.rows), BF),
            pltpu.VMEM((dm.width, dm.rows), BF),
            pltpu.VMEM((span, dm.rows), BF),
            pltpu.VMEM((2, dm.block, dm.score_tile), F32),
            pltpu.VMEM((2, dm.block, dm.grad_tile), BF),
            pltpu.VMEM((dm.slots, dm.rows), F32),
            pltpu.VMEM((dm.slots, dm.rows), F32),
            pltpu.VMEM((dm.slots, dm.rows), F32),
            pltpu.VMEM((dm.width, dm.rows), F32),
            pltpu.VMEM((dm.slots,) + terms, BF),
            pltpu.VMEM((2 * w,) + terms, BF),
            pltpu.VMEM(terms, F32),
            pltpu.VMEM((n, 2, dm.tokens, dm.width), BF),
            pltpu.VMEM((n, 2, dm.tokens, dm.width), BF),
            pltpu.VMEM(chunked, BF),
            dma((11,)),
        ]
        + [dma((2, n))] * 2
        + [dma((n,))] * 10
        + [dma((2, 8)), dma((2, dm.slots)), dma((8,)), dma((8,))],
        compiler_params=pltpu.CompilerParams(
            collective_id=0, has_side_effects=True, vmem_limit_bytes=63 * 2**20
        ),
        name="banded_attention_gradients",
    )(
        query,
        dout,
        output,
        keys.reshape(flat, dm.width),
        values.reshape(flat, dm.width),
    )


def solution(mesh):
    def on_device(query, keys, values, output, dout):
        dm = Dims(query, keys, mesh)
        dquery, dkeys, dvalues = fused(dm, query, keys, values, output, dout)
        return dquery, dkeys.reshape(keys.shape), dvalues.reshape(values.shape)

    spec = P(("blk", "head"), None, None)
    return jax.shard_map(
        on_device, mesh=mesh, in_specs=(spec,) * 5, out_specs=(spec,) * 3, check_vma=False
    )
```
